32 devices in a mesh: groups: 2 (over x), tm: 8 (over z, y), head: 2 (over core).
Axes of the slice: x: 2, y: 2, z: 4, core: 2. Of those that a mesh axis runs over, the one named last changes fastest.
Arguments:
- spectrogram: bfloat16 [512, 4, 1024], P(('groups', 'tm')), parts along dimension 0, may hold values from -6 to 6
- band_lengths: int32 [64], replicated, may hold values from 1 to 32, 1024 in all
- band_weight: bfloat16 [64, 128, 384], P('head'), may hold values from -0.75 to 0.75
- attn_weights: bfloat16 [2, 4, 384, 384], replicated, may hold values from -2 to 2
- ff_in: bfloat16 [2, 384, 1536], replicated, may hold values from -0.3125 to 0.3125
- ff_out: bfloat16 [2, 1536, 384], replicated, may hold values from -0.15625 to 0.15625
Outputs:
- separated: bfloat16 [512, 64, 384], P(('groups', 'tm'), 'head'), parts along dimension 0
The draws below stay inside these ranges and needn't reach their ends.
There are 2 independent parts, one for each index of `groups`. The reference program is written for one: setup_inputs(seed, part) draws one part's arguments, and reference() takes and returns one part's arrays. A program takes and returns all parts, laid end to end along the dimension named above; an argument that names none is the same for every part. Nothing has to cross between parts.
Inputs may be any that keep to these rules, and one draw needn't show every extreme that they name: The bands cover the 1024 bins in order without gaps, so band_lengths sum to 1024.
All inputs are finite; a program needn't handle non-finite values.
Results may differ from the reference program's by a relative error of at most 0.04.
Values may be sent and summed in bfloat16 or wider, within the bound.
No kernel may reach another device: no remote copies, remote signals or barrier semaphores. Data moves between devices by JAX's collectives and lax.ppermute only.
A program may use at most 128 MiB of HBM per device.

```python
import math
import jax
import jax.numpy as jnp
import numpy as np
from jax import lax

D = 384
HEADS = 8
HEAD_DIM = 48
FF = 1536
BANDS = 64
BINS = 1024
MAXW = 32
CH = 4
FRAMES = 256


def draw_attn_weights(key, part):
    base_key = jax.random.fold_in(jax.random.fold_in(key, 7), 0)
    base = jax.random.truncated_normal(base_key, -4.0, 4.0, (2, 4, D, D), jnp.float32) * D ** (-0.5)
    return jnp.clip(base, -2.0, 2.0).astype(jnp.bfloat16)


def block_scale(stream_key, dims, cuts, smallest, high):
    def one(dim, blocks):
        heights = jax.random.uniform(jax.random.fold_in(jax.random.fold_in(stream_key, 6), dim), (blocks,), jnp.float32, smallest / len(cuts), high / len(cuts))
        return jnp.repeat(jnp.exp(heights), dims[dim] // blocks).reshape((-1,) + (1,) * (len(dims) - dim - 1))

    loudness = one(*cuts[0])
    for cut in cuts[1:]:
        loudness = loudness * one(*cut)
    return loudness


def split_up(amount, total, reach, lean):
    portions = [(1 << 20) // math.isqrt(standing ** lean) + 1 for standing in range(2, amount + 1)]
    rest, holding = total - reach - (amount - 1), [1] * (amount - 1)
    while rest > 0:
        candidates = [i for i in range(amount - 1) if holding[i] < reach]
        pool, left = sum([portions[i] for i in candidates]), rest
        for i in candidates:
            more = min(reach - holding[i], max(1, left * portions[i] // pool), rest)
            holding[i] = holding[i] + more
            rest = rest - more
    return np.array([reach] + holding)


def ragged_sizes(key, number_of, total, reach, lean):
    if number_of == 2:
        one = jax.random.randint(key, (), max(1, total - reach), min(reach, total - 1) + 1)
        return jnp.stack([one, total - one])
    lengths = jnp.asarray(split_up(number_of, total, reach, lean), jnp.int32)
    couples = (number_of - 1) // 2
    donor, sink = lengths[1:1 + 2 * couples:2], lengths[2:2 + 2 * couples:2]
    room = jnp.minimum(donor - 1, reach - sink)
    shifted = jax.random.randint(jax.random.fold_in(key, 1), (couples,), 0, 1 << 20) % (room + 1)
    lengths = lengths.at[1:1 + 2 * couples:2].set(donor - shifted).at[2:2 + 2 * couples:2].set(sink + shifted)
    return lengths[jax.random.permutation(jax.random.fold_in(key, 2), number_of)]


def gaussian(rng, shape, width, reach, pieces=(), held_as=jnp.bfloat16):
    factor_of = block_scale(rng, shape, pieces, -0.22, 0.18) if pieces else 1.0
    result = jax.random.normal(rng, shape, jnp.float32) * width * factor_of
    return jnp.minimum(jnp.maximum(result, -reach), reach).astype(held_as)


def setup_inputs(seed: int = 0, part: int = 0) -> dict:
    splits = jax.random.split(jax.random.key(seed), 7)
    own_keys = jax.random.split(jax.random.fold_in(splits[6], part), 7)
    spectrogram = gaussian(own_keys[0], (FRAMES, CH, BINS), 1.0, 6.0, ((0, 8),))
    band_lengths = ragged_sizes(splits[1], BANDS, BINS, MAXW, 2).astype(jnp.int32)
    band_weight = gaussian(splits[2], (BANDS, CH * MAXW, D), (CH * MAXW // 2) ** -0.5, 0.75, ((0, 2),))
    attn_weights = draw_attn_weights(jax.random.fold_in(splits[6], 71), part)
    ff_in = gaussian(splits[4], (2, D, FF), D ** -0.5, 0.3125)
    ff_out = gaussian(splits[5], (2, FF, D), FF ** -0.5, 0.15625)
    return {"spectrogram": spectrogram, "band_lengths": band_lengths, "band_weight": band_weight, "attn_weights": attn_weights, "ff_in": ff_in, "ff_out": ff_out}


def rms_norm(stream):
    widened = stream.astype(jnp.float32)
    return (widened * lax.rsqrt(lax.optimization_barrier(jnp.mean(widened * widened, axis=-1, keepdims=True)) + 1e-06)).astype(jnp.bfloat16)

def rotate(tensor, position):
    full_shape = tensor.shape
    by_heads = tensor.reshape(full_shape[:-1] + (HEADS, HEAD_DIM))
    half_dim = HEAD_DIM // 2
    frequency = 10000.0 ** (-jnp.arange(half_dim, dtype=jnp.float32) / half_dim)
    angles = position[..., None, None] * frequency
    cosine = jnp.cos(angles)
    sine_part = jnp.sin(angles)
    first_half = by_heads[..., :half_dim]
    second_half = by_heads[..., half_dim:]
    turned = jnp.concatenate([first_half * cosine - second_half * sine_part, second_half * cosine + first_half * sine_part], axis=-1)
    return turned.reshape(full_shape)

def attend(queries, key_rows, value_rows, heads):
    full_shape = queries.shape
    head_width = full_shape[-1] // heads
    query_heads = queries.astype(jnp.float32).reshape(full_shape[:-1] + (heads, head_width))
    key_heads = key_rows.astype(jnp.float32).reshape(key_rows.shape[:-1] + (heads, head_width))
    value_heads = value_rows.astype(jnp.float32).reshape(value_rows.shape[:-1] + (heads, head_width))
    scores = jnp.einsum('...qhd,...khd->...hqk', query_heads, key_heads) * head_width ** (-0.5)
    highest = lax.optimization_barrier(jnp.max(scores, axis=-1, keepdims=True))
    exponent = jnp.exp(scores - highest)
    weights = (exponent / lax.optimization_barrier(jnp.sum(exponent, axis=-1, keepdims=True))).astype(jnp.bfloat16)
    mixed = jnp.einsum('...hqk,...khd->...qhd', weights.astype(jnp.float32), value_heads)
    return mixed.reshape(full_shape).astype(jnp.bfloat16)

def project(normed, position, layer_weights):
    queries = rotate(jnp.dot(normed, layer_weights[0], preferred_element_type=jnp.float32), position).astype(jnp.bfloat16)
    key_rows = rotate(jnp.dot(normed, layer_weights[1], preferred_element_type=jnp.float32), position).astype(jnp.bfloat16)
    value_rows = jnp.dot(normed, layer_weights[2], preferred_element_type=jnp.float32).astype(jnp.bfloat16)
    return (queries, key_rows, value_rows)

def finish(stream, attended, out_weight, up_weight, down_weight):
    after = (stream.astype(jnp.float32) + jnp.dot(attended, out_weight, preferred_element_type=jnp.float32)).astype(jnp.bfloat16)
    hidden = jax.nn.gelu(jnp.dot(rms_norm(after), up_weight, preferred_element_type=jnp.float32), approximate=False).astype(jnp.bfloat16)
    return (after.astype(jnp.float32) + jnp.dot(hidden, down_weight, preferred_element_type=jnp.float32)).astype(jnp.bfloat16)

def transform(stream, position, layer_weights, up_weight, down_weight):
    queries, key_rows, value_rows = project(rms_norm(stream), position, layer_weights)
    attended = attend(queries, key_rows, value_rows, HEADS)
    return finish(stream, attended, layer_weights[3], up_weight, down_weight)

def reference(spectrogram, band_lengths, band_weight, attn_weights, ff_in, ff_out):
    starts = (jnp.cumsum(band_lengths) - band_lengths).astype(jnp.int32)
    offsets = jnp.arange(MAXW, dtype=jnp.int32)
    index_table = jnp.minimum(starts[:, None] + offsets[None, :], BINS - 1).astype(jnp.int32)
    live = offsets[None, :] < band_lengths[:, None]
    picked = spectrogram[:, :, index_table]
    picked = jnp.where(live[None, None], picked, jnp.zeros_like(picked))
    features = picked.transpose(0, 2, 1, 3).reshape(FRAMES, BANDS, CH * MAXW).astype(jnp.float32)
    square_mean = lax.optimization_barrier(jnp.sum(features * features, axis=-1)) / (CH * band_lengths).astype(jnp.float32)
    normed = (features * lax.rsqrt(jnp.maximum(square_mean, 0.25))[..., None]).astype(jnp.bfloat16)
    stream = jnp.einsum('fbc,bcd->fbd', normed.astype(jnp.float32), band_weight.astype(jnp.float32)).astype(jnp.bfloat16)
    frame_pos = jnp.arange(FRAMES, dtype=jnp.float32)
    columns = lax.map(lambda column: transform(column, frame_pos, attn_weights[0], ff_in[0], ff_out[0]), stream.transpose(1, 0, 2))
    stream = columns.transpose(1, 0, 2)
    band_pos = jnp.arange(BANDS, dtype=jnp.float32)
    return transform(stream, band_pos, attn_weights[1], ff_in[1], ff_out[1])
```

```python
import functools
import math

import jax
import jax.numpy as jnp
import numpy as np
from jax import lax
from jax.experimental import pallas as pl
from jax.experimental.pallas import tpu as pltpu
from jax.sharding import PartitionSpec as P

HEADS = 8
HEAD_DIM = 48
MAXW = 32
CH = 4
HALF = HEAD_DIM // 2
HPAD = 32
VPAD = 64
LANES = 128
PER = LANES // HPAD
CHUNKS = HEADS // PER
QW = 2 * HEADS * HPAD
VW = HEADS * VPAD
CW = 2 * LANES
BSTEP = 8
BF = jnp.bfloat16
F32 = jnp.float32


def mm(a, b):
    return jnp.dot(a, b, preferred_element_type=F32)


def mm_nt(a, b):
    return lax.dot_general(a, b, (((1,), (1,)), ((), ())), preferred_element_type=F32)


def rms(x):
    return (x * lax.rsqrt(jnp.mean(x * x, axis=-1, keepdims=True) + 1e-06)).astype(BF)


def tables(count):
    freq = 10000.0 ** (-np.arange(HALF, dtype=np.float64) / HALF)
    angle = np.arange(count, dtype=np.float64)[:, None] * freq
    pad = ((0, 0), (0, HPAD - HALF))
    cosine = np.tile(np.pad(np.cos(angle), pad), (1, PER))
    sine = np.tile(np.pad(np.sin(angle), pad), (1, PER))
    return np.concatenate([cosine, sine], axis=1).astype(np.float32)


def rotated(x, table, c):
    period = table.shape[0]
    u = x[:, c * CW : c * CW + LANES].reshape(-1, period, LANES)
    w = x[:, c * CW + LANES : (c + 1) * CW].reshape(-1, period, LANES)
    cosine, sine = table[None, :, :LANES], table[None, :, LANES:]
    first = (u * cosine - w * sine).reshape(-1, LANES).astype(BF)
    second = (w * cosine + u * sine).reshape(-1, LANES).astype(BF)
    return first, second


def gelu(x):
    a = jnp.abs(x)
    t = 1.0 / (1.0 + (0.3275911 * math.sqrt(0.5)) * a)
    poly = t * (
        0.5 * 0.254829592
        + t
        * (
            0.5 * -0.284496736
            + t * (0.5 * 1.421413741 + t * (0.5 * -1.453152027 + t * (0.5 * 1.061405429)))
        )
    )
    tail = poly * jnp.exp2((x * x) * (-0.5 * math.log2(math.e)))
    return jnp.maximum(x, 0.0) - a * tail


def finish(stream, att, wo, w1, w2, hid_ref):
    mid = stream + mm(att, wo[...])
    normed = rms(mid)
    width = w1.shape[-1]
    step = 256
    for j in range(0, width, step):
        hid_ref[:, j : j + step] = gelu(mm(normed, w1[:, j : j + step])).astype(BF)
    return mid + mm(hid_ref[...], w2[...])


def heads_attend(q4, k4, v4):
    m = q4.shape[0]
    lane = lax.broadcasted_iota(jnp.int32, (1, CW), 1)
    own = (lane % LANES) // HPAD
    stacked = jnp.concatenate(
        [jnp.where(own == h, q4, jnp.zeros_like(q4)) for h in range(PER)], axis=0
    )
    s = mm_nt(stacked, k4)
    p = jnp.exp2(s - jnp.max(s, axis=-1, keepdims=True))
    inv = 1.0 / jnp.sum(p, axis=-1, keepdims=True)
    r = mm(p.astype(BF), v4) * inv
    vlane = lax.broadcasted_iota(jnp.int32, (1, PER * VPAD), 1) // VPAD
    out = r[:m]
    for h in range(1, PER):
        out = jnp.where(vlane == h, r[h * m : (h + 1) * m], out)
    return out


def prep_kernel(w_ref, wq_ref, wkv_ref, wo_ref):
    d = w_ref.shape[-1]
    row = lax.broadcasted_iota(jnp.int32, (d, QW), 0)
    col = lax.broadcasted_iota(jnp.int32, (d, QW), 1)
    inner = col % HPAD
    head = (col // CW) * PER + (col % LANES) // HPAD
    source = head * HEAD_DIM + ((col % CW) // LANES) * HALF + inner
    pick = jnp.where((row == source) & (inner < HALF), 1.0, 0.0).astype(BF)
    vcol = lax.broadcasted_iota(jnp.int32, (d, VW), 1)
    vrow = lax.broadcasted_iota(jnp.int32, (d, VW), 0)
    vpick = jnp.where(
        (vrow == (vcol // VPAD) * HEAD_DIM + vcol % VPAD) & (vcol % VPAD < HEAD_DIM), 1.0, 0.0
    ).astype(BF)
    orow = lax.broadcasted_iota(jnp.int32, (VW, d), 0)
    ocol = lax.broadcasted_iota(jnp.int32, (VW, d), 1)
    opick = jnp.where(
        (ocol == (orow // VPAD) * HEAD_DIM + orow % VPAD) & (orow % VPAD < HEAD_DIM), 1.0, 0.0
    ).astype(BF)
    wq_ref[0] = mm(w_ref[0, 0], pick).astype(BF)
    wkv_ref[0, :, :QW] = mm(w_ref[0, 1], pick).astype(BF)
    wkv_ref[0, :, QW:] = mm(w_ref[0, 2], vpick).astype(BF)
    wo_ref[0] = mm(opick, w_ref[0, 3]).astype(BF)


def prep(attn_weights):
    layers, _, d, _ = attn_weights.shape
    return pl.pallas_call(
        prep_kernel,
        grid=(layers,),
        in_specs=[pl.BlockSpec((1, 4, d, d), lambda i: (i, 0, 0, 0))],
        out_specs=[
            pl.BlockSpec((1, d, QW), lambda i: (i, 0, 0)),
            pl.BlockSpec((1, d, QW + VW), lambda i: (i, 0, 0)),
            pl.BlockSpec((1, VW, d), lambda i: (i, 0, 0)),
        ],
        out_shape=[
            jax.ShapeDtypeStruct((layers, d, QW), BF),
            jax.ShapeDtypeStruct((layers, d, QW + VW), BF),
            jax.ShapeDtypeStruct((layers, VW, d), BF),
        ],
        cost_estimate=pl.CostEstimate(
            flops=layers * 8 * d * d * QW, bytes_accessed=layers * 16 * d * d, transcendentals=0
        ),
        name="prep",
    )(attn_weights)


def embed_block(x_ref, weight_ref, lens, starts, bins):
    frames = x_ref.shape[0] // CH
    group = LANES // MAXW
    pieces = []
    lane = lax.broadcasted_iota(jnp.int32, (1, LANES), 1)
    for g in range(BSTEP // group):
        ids = range(g * group, (g + 1) * group)
        base = jnp.minimum(starts[g * group] // LANES, (bins - 2 * LANES) // LANES) * LANES
        base = pl.multiple_of(base, LANES)
        window = x_ref[:, pl.ds(base, 2 * LANES)]
        target = jnp.full((1, LANES), -1, jnp.int32)
        width = jnp.zeros((1, LANES), F32)
        for k, b in enumerate(ids):
            mine = (lane // MAXW == k) & (lane % MAXW < lens[b])
            target = jnp.where(mine, starts[b] - base + lane % MAXW, target)
        bin_row = lax.broadcasted_iota(jnp.int32, (2 * LANES, LANES), 0)
        select = jnp.where(bin_row == target, 1.0, 0.0).astype(BF)
        picked = mm(window, select)
        square = picked * picked
        total = square[:frames]
        for c in range(1, CH):
            total = total + square[c * frames : (c + 1) * frames]
        left, scales, weights = [], [], []
        narrow = picked.astype(BF)
        for k, b in enumerate(ids):
            mine = lane // MAXW == k
            mean = jnp.sum(jnp.where(mine, total, 0.0), axis=-1, keepdims=True) / (
                (CH * lens[b]).astype(F32)
            )
            scales.append(lax.rsqrt(jnp.maximum(mean, 0.25)))
            left.append(
                jnp.concatenate(
                    [
                        jnp.where(mine, narrow[c * frames : (c + 1) * frames], jnp.zeros((), BF))
                        for c in range(CH)
                    ],
                    axis=1,
                )
            )
        weight = jnp.concatenate(
            [weight_ref[b, c * MAXW : (c + 1) * MAXW, :] for c in range(CH) for b in ids], axis=0
        )
        pieces.append(
            mm(jnp.concatenate(left, axis=0), weight) * jnp.concatenate(scales, axis=0)
        )
    return jnp.concatenate(pieces, axis=0)


def band_scalars(meta, lens_ref, bands_dev):
    first = meta[0] * bands_dev + pl.program_id(0) * BSTEP
    start = lax.fori_loop(0, first, lambda i, acc: acc + lens_ref[i], jnp.int32(0))
    lens, starts = [], []
    for b in range(BSTEP):
        lens.append(lens_ref[first + b])
        starts.append(start)
        start = start + lens[-1]
    return lens, starts


def kv_kernel(blocks, slots, bands_dev, with_q, meta, lens_ref, table_ref, *refs):
    x_refs, refs = refs[:blocks], refs[blocks:]
    weight_ref, wkv_ref, *refs = refs
    if with_q:
        wq_ref, *refs = refs
    kv_ref = refs[0]
    lens, starts = band_scalars(meta, lens_ref, bands_dev)
    bins = x_refs[0].shape[1]
    frames = x_refs[0].shape[0] // CH
    for i in range(blocks):
        stream = embed_block(x_refs[i], weight_ref, lens, starts, bins)
        normed = rms(stream)
        kv = mm(normed, wkv_ref[0])
        place = pl.multiple_of(meta[slots[i]] * frames, frames)
        table = table_ref[pl.ds(place, frames), :]

        def put(ref, cols, value, width):
            value = value.reshape(BSTEP, frames, width)
            if len(ref.shape) == 4:
                ref[:, i, :, cols : cols + width] = value
            else:
                ref[:, :, cols : cols + width] = value

        for c in range(CHUNKS):
            first, second = rotated(kv, table, c)
            put(kv_ref, c * CW, first, LANES)
            put(kv_ref, c * CW + LANES, second, LANES)
        put(kv_ref, QW, kv[:, QW:].astype(BF), VW)
        if with_q:
            q_ref, stream_ref = refs[1:]
            q = mm(normed, wq_ref[0])
            scaled = table * (HEAD_DIM**-0.5 * math.log2(math.e))
            for c in range(CHUNKS):
                first, second = rotated(q, scaled, c)
                put(q_ref, c * CW, first, LANES)
                put(q_ref, c * CW + LANES, second, LANES)
            put(stream_ref, 0, stream.astype(BF), stream.shape[1])


def keys_values(xs, slots, meta, band_lengths, table, band_weight, wkv, wq=None):
    blocks = len(xs)
    with_q = wq is not None
    rows, bins = xs[0].shape
    frames = rows // CH
    bands_dev, feat, d = band_weight.shape
    kvw = QW + VW
    lead = () if blocks == 1 else (blocks,)
    zeros = (0,) * (len(lead) + 2)
    out_shape = [jax.ShapeDtypeStruct((bands_dev,) + lead + (frames, kvw), BF)]
    out_specs = [pl.BlockSpec((BSTEP,) + lead + (frames, kvw), lambda i, *_: (i,) + zeros)]
    whole = lambda shape: pl.BlockSpec(shape, lambda i, *_: (0,) * len(shape))
    in_specs = [whole(table.shape)] + [whole((rows, bins))] * blocks
    in_specs += [
        pl.BlockSpec((BSTEP, feat, d), lambda i, *_: (i, 0, 0)),
        pl.BlockSpec((1, d, kvw), lambda i, *_: (0, 0, 0)),
    ]
    args = [table, *xs, band_weight, wkv]
    if with_q:
        in_specs.append(pl.BlockSpec((1, d, QW), lambda i, *_: (0, 0, 0)))
        args.append(wq)
        for width in (QW, d):
            out_shape.append(jax.ShapeDtypeStruct((bands_dev, frames, width), BF))
            out_specs.append(pl.BlockSpec((BSTEP, frames, width), lambda i, *_: (i, 0, 0)))
    tokens = blocks * frames * bands_dev
    return pl.pallas_call(
        functools.partial(kv_kernel, blocks, slots, bands_dev, with_q),
        grid_spec=pltpu.PrefetchScalarGridSpec(
            num_scalar_prefetch=2,
            grid=(bands_dev // BSTEP,),
            in_specs=in_specs,
            out_specs=out_specs,
        ),
        out_shape=out_shape,
        cost_estimate=pl.CostEstimate(
            flops=2 * tokens * d * (kvw + 4 * feat),
            bytes_accessed=2 * (tokens * kvw + d * kvw + bands_dev * feat * d),
            transcendentals=0,
        ),
        name="keys_values",
    )(meta, band_lengths, *args)


def time_kernel(parts, q_ref, stream_ref, *refs):
    kv_refs, refs = refs[:parts], refs[parts:]
    wo_ref, w1_ref, w2_ref, out_ref, att_ref, hid_ref = refs
    frames = q_ref.shape[1]
    for b in range(BSTEP):
        for c in range(CHUNKS):
            k4 = jnp.concatenate(
                [r[b, ..., c * CW : (c + 1) * CW].reshape(-1, CW) for r in kv_refs], axis=0
            )
            lo = QW + c * PER * VPAD
            v4 = jnp.concatenate(
                [r[b, ..., lo : lo + PER * VPAD].reshape(-1, PER * VPAD) for r in kv_refs], axis=0
            )
            out = heads_attend(q_ref[b, :, c * CW : (c + 1) * CW], k4, v4)
            att_ref[b * frames : (b + 1) * frames, c * PER * VPAD : (c + 1) * PER * VPAD] = (
                out.astype(BF)
            )
    stream = stream_ref[...].reshape(BSTEP * frames, -1).astype(F32)
    out = finish(stream, att_ref[...], wo_ref.at[0], w1_ref.at[0], w2_ref.at[0], hid_ref)
    out_ref[...] = out.astype(BF).reshape(out_ref.shape)


def time_layer(q, stream, kvs, wo, ff_in, ff_out):
    bands_dev, frames, d = stream.shape
    ff = ff_in.shape[-1]

    def band_block(shape):
        return pl.BlockSpec((BSTEP,) + shape[1:], lambda i: (i,) + (0,) * (len(shape) - 1))

    layer = lambda a: pl.BlockSpec((1,) + a.shape[1:], lambda i: (0, 0, 0))
    tokens = bands_dev * frames
    return pl.pallas_call(
        functools.partial(time_kernel, len(kvs)),
        grid=(bands_dev // BSTEP,),
        in_specs=[band_block(q.shape), band_block(stream.shape)]
        + [band_block(a.shape) for a in kvs]
        + [layer(wo), layer(ff_in), layer(ff_out)],
        out_specs=band_block(stream.shape),
        out_shape=jax.ShapeDtypeStruct(stream.shape, BF),
        scratch_shapes=[
            pltpu.VMEM((BSTEP * frames, VW), BF),
            pltpu.VMEM((BSTEP * frames, ff), BF),
        ],
        cost_estimate=pl.CostEstimate(
            flops=4 * tokens * d * (ff + d), bytes_accessed=16 * tokens * d, transcendentals=0
        ),
        name="time_layer",
    )(q, stream, *kvs, wo, ff_in, ff_out)


FSTEP = 8


def band_kernel(meta, table_ref, own_ref, far_ref, *refs):
    wq_ref, wkv_ref, wo_ref, w1_ref, w2_ref, out_ref, own32, far32, att_ref, hid_ref = refs
    bands, frames, d = own_ref.shape

    @pl.when(pl.program_id(0) == 0)
    def _():
        for source, wide in ((own_ref, own32), (far_ref, far32)):
            for j in range(d // LANES):
                part = source[:, :, j * LANES : (j + 1) * LANES].astype(F32)
                wide[j] = part.reshape(bands * frames, LANES)

    f0 = pl.program_id(0) * FSTEP

    def rows(wide):
        parts = [
            jnp.concatenate(
                [wide[j, pl.ds(f0 + f, bands, stride=frames), :] for f in range(FSTEP)], axis=0
            )
            for j in range(d // LANES)
        ]
        return jnp.concatenate(parts, axis=1)

    stream = rows(own32)
    n_own = rms(stream)
    n_far = rms(rows(far32))
    kv_own = mm(n_own, wkv_ref[0])
    kv_far = mm(n_far, wkv_ref[0])
    q = mm(n_own, wq_ref[0])
    t_own = table_ref[pl.ds(pl.multiple_of(meta[0] * bands, bands), bands), :]
    t_far = table_ref[pl.ds(pl.multiple_of((1 - meta[0]) * bands, bands), bands), :]
    t_q = t_own * (HEAD_DIM**-0.5 * math.log2(math.e))
    for c in range(CHUNKS):
        both = lambda x, t: jnp.concatenate(rotated(x, t, c), axis=1)
        k_own, k_far, q_c = both(kv_own, t_own), both(kv_far, t_far), both(q, t_q)
        lo = QW + c * PER * VPAD
        v_own = kv_own[:, lo : lo + PER * VPAD].astype(BF)
        v_far = kv_far[:, lo : lo + PER * VPAD].astype(BF)
        for f in range(FSTEP):
            at = slice(f * bands, (f + 1) * bands)
            out = heads_attend(
                q_c[at],
                jnp.concatenate([k_own[at], k_far[at]], axis=0),
                jnp.concatenate([v_own[at], v_far[at]], axis=0),
            )
            att_ref[at, c * PER * VPAD : (c + 1) * PER * VPAD] = out.astype(BF)
    out = finish(stream, att_ref[...], wo_ref.at[0], w1_ref.at[0], w2_ref.at[0], hid_ref)
    out_ref[...] = out.astype(BF).reshape(out_ref.shape)


def band_layer(own, far, meta, table, wq, wkv, wo, ff_in, ff_out):
    bands, frames, d = own.shape
    ff = ff_in.shape[-1]
    whole = lambda a: pl.BlockSpec(a.shape, lambda i, *_: (0,) * len(a.shape))
    layer = lambda a: pl.BlockSpec((1,) + a.shape[1:], lambda i, *_: (1, 0, 0))
    tokens = bands * frames
    return pl.pallas_call(
        band_kernel,
        grid_spec=pltpu.PrefetchScalarGridSpec(
            num_scalar_prefetch=1,
            grid=(frames // FSTEP,),
            in_specs=[whole(table), whole(own), whole(far)]
            + [layer(a) for a in (wq, wkv, wo, ff_in, ff_out)],
            out_specs=pl.BlockSpec((FSTEP, bands, d), lambda i, *_: (i, 0, 0)),
            scratch_shapes=[
                pltpu.VMEM((d // LANES, bands * frames, LANES), F32),
                pltpu.VMEM((d // LANES, bands * frames, LANES), F32),
                pltpu.VMEM((bands * FSTEP, VW), BF),
                pltpu.VMEM((bands * FSTEP, ff), BF),
            ],
        ),
        out_shape=jax.ShapeDtypeStruct((frames, bands, d), BF),
        cost_estimate=pl.CostEstimate(
            flops=4 * tokens * d * (ff + 3 * d), bytes_accessed=16 * tokens * d, transcendentals=0
        ),
        name="band_layer",
    )(meta, table, own, far, wq, wkv, wo, ff_in, ff_out)


def per_device(n, spectrogram, band_lengths, band_weight, attn_weights, ff_in, ff_out):
    frames, _, bins = spectrogram.shape
    bands_dev = band_weight.shape[0]
    order = list(range(0, n, 2)) + [i for i in range(n - 1, -1, -1) if i % 2]
    spot = {t: i for i, t in enumerate(order)}
    after = {t: order[(spot[t] + 1) % n] for t in order}
    before = {t: order[(spot[t] - 1) % n] for t in order}
    steps = n // 2
    book = np.zeros((n, 2, 2 + 2 * steps), np.int32)
    for t in range(n):
        for h in range(2):
            book[t, h, 0], book[t, h, 1] = h, t
            for s in range(1, steps + 1):
                sides = (order[(spot[t] - s) % n], order[(spot[t] + s) % n])
                book[t, h, 2 * s], book[t, h, 2 * s + 1] = sides[h], sides[1 - h]
    meta = lax.dynamic_slice(
        jnp.asarray(book),
        (lax.axis_index("tm"), lax.axis_index("head"), 0),
        (1, 1, book.shape[2]),
    ).reshape(-1)
    table = jnp.asarray(tables(n * frames))
    band_table = jnp.asarray(tables(2 * bands_dev))
    ring = [(2 * t, 2 * after[t]) for t in range(n)] + [
        (2 * t + 1, 2 * before[t] + 1) for t in range(n)
    ]
    swap = [(0, 1), (1, 0)]

    block = spectrogram.transpose(1, 0, 2).reshape(CH * frames, bins)
    wq, wkv, wo = prep(attn_weights)
    kv, q, stream = keys_values(
        [block], (1,), meta, band_lengths, table, band_weight, wkv, wq
    )
    kvs = [kv]
    held = block
    for s in range(1, steps + 1):
        held = lax.ppermute(held, ("tm", "head"), ring)
        xs, slots = [held], [2 * s]
        if 2 * s != n:
            xs.append(lax.ppermute(held, "head", swap))
            slots.append(2 * s + 1)
        kvs += keys_values(xs, tuple(slots), meta, band_lengths, table, band_weight, wkv)
    own = time_layer(q, stream, kvs, wo, ff_in, ff_out)
    far = lax.ppermute(own, "head", swap)
    return band_layer(own, far, meta, band_table, wq, wkv, wo, ff_in, ff_out)


def solution(mesh):
    return jax.shard_map(
        functools.partial(per_device, mesh.shape["tm"]),
        mesh=mesh,
        in_specs=(P(("groups", "tm"), None, None), P(), P("head", None, None), P(), P(), P()),
        out_specs=P(("groups", "tm"), "head", None),
        check_vma=False,
    )
```

```python
import functools
import math

import jax
import jax.numpy as jnp
import numpy as np
from jax import lax
from jax.experimental import pallas as pl
from jax.experimental.pallas import tpu as pltpu
from jax.sharding import PartitionSpec as P

HEADS = 8
HEAD_DIM = 48
MAXW = 32
CH = 4
HALF = HEAD_DIM // 2
HPAD = 32
VPAD = 64
LANES = 128
PER = LANES // HPAD
CHUNKS = HEADS // PER
QW = 2 * HEADS * HPAD
VW = HEADS * VPAD
GROUP = LANES // MAXW
CW = 2 * LANES
BSTEP = 8
BATCH = 8
BF = jnp.bfloat16
F32 = jnp.float32


def mm(a, b):
    return jnp.dot(a, b, preferred_element_type=F32)


def mm_nt(a, b):
    return lax.dot_general(a, b, (((1,), (1,)), ((), ())), preferred_element_type=F32)


def rms(x):
    return (x * lax.rsqrt(jnp.mean(x * x, axis=-1, keepdims=True) + 1e-06)).astype(BF)


def tables(count):
    freq = 10000.0 ** (-np.arange(HALF, dtype=np.float64) / HALF)
    angle = np.arange(count, dtype=np.float64)[:, None] * freq
    pad = ((0, 0), (0, HPAD - HALF))
    cosine = np.tile(np.pad(np.cos(angle), pad), (1, PER))
    sine = np.tile(np.pad(np.sin(angle), pad), (1, PER))
    return np.concatenate([cosine, sine], axis=1).astype(np.float32)


def rotated(x, table, c):
    period = table.shape[0]
    u = x[:, c * CW : c * CW + LANES].reshape(-1, period, LANES)
    w = x[:, c * CW + LANES : (c + 1) * CW].reshape(-1, period, LANES)
    cosine, sine = table[None, :, :LANES], table[None, :, LANES:]
    first = (u * cosine - w * sine).reshape(-1, LANES).astype(BF)
    second = (w * cosine + u * sine).reshape(-1, LANES).astype(BF)
    return first, second


def gelu(x):
    return 0.5 * x * (1.0 + lax.erf(x * math.sqrt(0.5)))


def finish(stream, att, wo, w1, w2, hid_ref):
    mid = stream + mm(att, wo[...])
    normed = rms(mid)
    width = w1.shape[-1]
    step = 256
    for j in range(0, width, step):
        hid_ref[:, j : j + step] = gelu(mm(normed, w1[:, j : j + step])).astype(BF)
    return mid + mm(hid_ref[...], w2[...])


def attend(queries, keys, values):
    m = queries[0].shape[0]
    own = (lax.broadcasted_iota(jnp.int32, (1, CW), 1) % LANES) // HPAD
    vlane = lax.broadcasted_iota(jnp.int32, (1, PER * VPAD), 1) // VPAD
    stacked = [
        jnp.concatenate([jnp.where(own == h, q, jnp.zeros_like(q)) for h in range(PER)], axis=0)
        for q in queries
    ]
    scores = [mm_nt(q, k) for q, k in zip(stacked, keys)]
    highest = [jnp.max(s, axis=-1, keepdims=True) for s in scores]
    powers = [jnp.exp2(s - h) for s, h in zip(scores, highest)]
    sums = [jnp.sum(p, axis=-1, keepdims=True) for p in powers]
    mixed = [mm(p.astype(BF), v) for p, v in zip(powers, values)]
    outs = []
    for r, total in zip(mixed, sums):
        r = r * (1.0 / total)
        out = r[:m]
        for h in range(1, PER):
            out = jnp.where(vlane == h, r[h * m : (h + 1) * m], out)
        outs.append(out.astype(BF))
    return outs


def prep_kernel(w_ref, wq_ref, wkv_ref, wo_ref):
    d = w_ref.shape[-1]
    row = lax.broadcasted_iota(jnp.int32, (d, QW), 0)
    col = lax.broadcasted_iota(jnp.int32, (d, QW), 1)
    inner = col % HPAD
    head = (col // CW) * PER + (col % LANES) // HPAD
    source = head * HEAD_DIM + ((col % CW) // LANES) * HALF + inner
    pick = jnp.where((row == source) & (inner < HALF), 1.0, 0.0).astype(BF)
    vcol = lax.broadcasted_iota(jnp.int32, (d, VW), 1)
    vrow = lax.broadcasted_iota(jnp.int32, (d, VW), 0)
    vpick = jnp.where(
        (vrow == (vcol // VPAD) * HEAD_DIM + vcol % VPAD) & (vcol % VPAD < HEAD_DIM), 1.0, 0.0
    ).astype(BF)
    orow = lax.broadcasted_iota(jnp.int32, (VW, d), 0)
    ocol = lax.broadcasted_iota(jnp.int32, (VW, d), 1)
    opick = jnp.where(
        (ocol == (orow // VPAD) * HEAD_DIM + orow % VPAD) & (orow % VPAD < HEAD_DIM), 1.0, 0.0
    ).astype(BF)
    wq_ref[0] = mm(w_ref[0, 0], pick).astype(BF)
    wkv_ref[0, :, :QW] = mm(w_ref[0, 1], pick).astype(BF)
    wkv_ref[0, :, QW:] = mm(w_ref[0, 2], vpick).astype(BF)
    wo_ref[0] = mm(opick, w_ref[0, 3]).astype(BF)


def prep(attn_weights):
    layers, _, d, _ = attn_weights.shape
    return pl.pallas_call(
        prep_kernel,
        grid=(layers,),
        in_specs=[pl.BlockSpec((1, 4, d, d), lambda i: (i, 0, 0, 0))],
        out_specs=[
            pl.BlockSpec((1, d, QW), lambda i: (i, 0, 0)),
            pl.BlockSpec((1, d, QW + VW), lambda i: (i, 0, 0)),
            pl.BlockSpec((1, VW, d), lambda i: (i, 0, 0)),
        ],
        out_shape=[
            jax.ShapeDtypeStruct((layers, d, QW), BF),
            jax.ShapeDtypeStruct((layers, d, QW + VW), BF),
            jax.ShapeDtypeStruct((layers, VW, d), BF),
        ],
        cost_estimate=pl.CostEstimate(
            flops=layers * 8 * d * d * QW, bytes_accessed=layers * 16 * d * d, transcendentals=0
        ),
        compiler_params=pltpu.CompilerParams(vmem_limit_bytes=24 << 20),
        name="prep",
    )(attn_weights)


def embed(x_refs, weight_ref, lens, starts):
    rows, bins = x_refs[0].shape
    frames = rows // CH
    lane = lax.broadcasted_iota(jnp.int32, (1, LANES), 1)
    inner = lane % MAXW
    bin_row = lax.broadcasted_iota(jnp.int32, (2 * LANES, LANES), 0)
    groups = [range(b, b + GROUP) for b in range(0, BSTEP, GROUP)]
    picked = []
    for ids in groups:
        base = jnp.minimum(starts[ids[0]] // LANES, (bins - 2 * LANES) // LANES) * LANES
        base = pl.multiple_of(base, LANES)
        target = jnp.full((1, LANES), -1, jnp.int32)
        for k, b in enumerate(ids):
            mine = (lane // MAXW == k) & (inner < lens[b])
            target = jnp.where(mine, starts[b] - base + inner, target)
        select = jnp.where(bin_row == target, 1.0, 0.0).astype(BF)
        window = jnp.concatenate([x[:, pl.ds(base, 2 * LANES)] for x in x_refs], axis=0)
        picked.append(mm(window, select))
    scales, lefts = [], []
    for ids, features in zip(groups, picked):
        narrow = features.astype(BF)
        square = features * features
        scale, left = [], []
        for i in range(len(x_refs)):
            spots = [slice(i * rows + c * frames, i * rows + (c + 1) * frames) for c in range(CH)]
            total = square[spots[0]]
            for spot in spots[1:]:
                total = total + square[spot]
            for k, b in enumerate(ids):
                mine = lane // MAXW == k
                mean = jnp.sum(jnp.where(mine, total, 0.0), axis=-1, keepdims=True) / (
                    (CH * lens[b]).astype(F32)
                )
                scale.append(lax.rsqrt(jnp.maximum(mean, 0.25)))
                kept = [jnp.where(mine, narrow[spot], jnp.zeros((), BF)) for spot in spots]
                left.append(jnp.concatenate(kept, axis=1))
        scales.append(jnp.concatenate(scale, axis=0))
        lefts.append(jnp.concatenate(left, axis=0))
    streams = []
    for ids, left, scale in zip(groups, lefts, scales):
        weight = jnp.concatenate(
            [weight_ref[b, c * MAXW : (c + 1) * MAXW, :] for c in range(CH) for b in ids], axis=0
        )
        streams.append(mm(left, weight) * scale)
    return jnp.concatenate(streams, axis=0)


def band_scalars(meta, lens_ref, bands_dev):
    first = meta[0] * bands_dev + pl.program_id(0) * BSTEP
    start = lax.fori_loop(0, first, lambda i, acc: acc + lens_ref[i], jnp.int32(0))
    lens, starts = [], []
    for b in range(BSTEP):
        lens.append(lens_ref[first + b])
        starts.append(start)
        start = start + lens[-1]
    return lens, starts


def kv_kernel(blocks, slots, bands_dev, with_q, meta, lens_ref, table_ref, *refs):
    x_refs, refs = refs[:blocks], refs[blocks:]
    weight_ref, wkv_ref, *refs = refs
    if with_q:
        wq_ref, *refs = refs
    kv_ref = refs[0]
    lens, starts = band_scalars(meta, lens_ref, bands_dev)
    frames = x_refs[0].shape[0] // CH
    stream = embed(x_refs, weight_ref, lens, starts)
    normed = rms(stream)
    kv = mm(normed, wkv_ref[0])
    places = [pl.multiple_of(meta[slot] * frames, frames) for slot in slots]
    table = jnp.concatenate(
        [table_ref[pl.ds(p, frames), :] for p in places for _ in range(GROUP)], axis=0
    )

    def put(ref, cols, value):
        width = value.shape[1]
        value = value.reshape(BSTEP // GROUP, blocks, GROUP, frames, width)
        for g in range(BSTEP // GROUP):
            bands = slice(g * GROUP, (g + 1) * GROUP)
            if len(ref.shape) == 3:
                ref[bands, :, cols : cols + width] = value[g, 0]
                continue
            for i in range(blocks):
                ref[bands, i, :, cols : cols + width] = value[g, i]

    for c in range(CHUNKS):
        first, second = rotated(kv, table, c)
        put(kv_ref, c * CW, first)
        put(kv_ref, c * CW + LANES, second)
    put(kv_ref, QW, kv[:, QW:].astype(BF))
    if with_q:
        q_ref, stream_ref = refs[1:]
        q = mm(normed, wq_ref[0])
        scaled = table * (HEAD_DIM**-0.5 * math.log2(math.e))
        for c in range(CHUNKS):
            first, second = rotated(q, scaled, c)
            put(q_ref, c * CW, first)
            put(q_ref, c * CW + LANES, second)
        put(stream_ref, 0, stream.astype(BF))


def keys_values(xs, slots, meta, band_lengths, table, band_weight, wkv, wq=None):
    blocks = len(xs)
    with_q = wq is not None
    rows, bins = xs[0].shape
    frames = rows // CH
    bands_dev, feat, d = band_weight.shape
    kvw = QW + VW
    lead = () if blocks == 1 else (blocks,)
    zeros = (0,) * (len(lead) + 2)
    out_shape = [jax.ShapeDtypeStruct((bands_dev,) + lead + (frames, kvw), BF)]
    out_specs = [pl.BlockSpec((BSTEP,) + lead + (frames, kvw), lambda i, *_: (i,) + zeros)]
    whole = lambda shape: pl.BlockSpec(shape, lambda i, *_: (0,) * len(shape))
    in_specs = [whole(table.shape)] + [whole((rows, bins))] * blocks
    in_specs += [
        pl.BlockSpec((BSTEP, feat, d), lambda i, *_: (i, 0, 0)),
        pl.BlockSpec((1, d, kvw), lambda i, *_: (0, 0, 0)),
    ]
    args = [table, *xs, band_weight, wkv]
    if with_q:
        in_specs.append(pl.BlockSpec((1, d, QW), lambda i, *_: (0, 0, 0)))
        args.append(wq)
        for width in (QW, d):
            out_shape.append(jax.ShapeDtypeStruct((bands_dev, frames, width), BF))
            out_specs.append(pl.BlockSpec((BSTEP, frames, width), lambda i, *_: (i, 0, 0)))
    tokens = blocks * frames * bands_dev
    return pl.pallas_call(
        functools.partial(kv_kernel, blocks, slots, bands_dev, with_q),
        grid_spec=pltpu.PrefetchScalarGridSpec(
            num_scalar_prefetch=2,
            grid=(bands_dev // BSTEP,),
            in_specs=in_specs,
            out_specs=out_specs,
        ),
        out_shape=out_shape,
        cost_estimate=pl.CostEstimate(
            flops=2 * tokens * d * (kvw + 4 * feat),
            bytes_accessed=2 * (tokens * kvw + d * kvw + bands_dev * feat * d),
            transcendentals=0,
        ),
        compiler_params=pltpu.CompilerParams(vmem_limit_bytes=24 << 20),
        name="keys_values",
    )(meta, band_lengths, *args)


def time_kernel(parts, q_ref, stream_ref, *refs):
    kv_refs, refs = refs[:parts], refs[parts:]
    wo_ref, w1_ref, w2_ref, out_ref, att_ref, hid_ref = refs
    frames = q_ref.shape[1]
    for c in range(CHUNKS):
        lo = QW + c * PER * VPAD

        def keyed(b, start, width):
            parts = [r[b, ..., start : start + width].reshape(-1, width) for r in kv_refs]
            return jnp.concatenate(parts, axis=0)

        for b0 in range(0, BSTEP, BATCH):
            ids = range(b0, b0 + BATCH)
            outs = attend(
                [q_ref[b, :, c * CW : (c + 1) * CW] for b in ids],
                [keyed(b, c * CW, CW) for b in ids],
                [keyed(b, lo, PER * VPAD) for b in ids],
            )
            for b, out in zip(ids, outs):
                att_ref[b * frames : (b + 1) * frames, c * PER * VPAD : (c + 1) * PER * VPAD] = out
    stream = stream_ref[...].reshape(BSTEP * frames, -1).astype(F32)
    out = finish(stream, att_ref[...], wo_ref.at[0], w1_ref.at[0], w2_ref.at[0], hid_ref)
    out_ref[...] = out.astype(BF).reshape(out_ref.shape)


def time_layer(q, stream, kvs, wo, ff_in, ff_out):
    bands_dev, frames, d = stream.shape
    ff = ff_in.shape[-1]

    def band_block(shape):
        return pl.BlockSpec((BSTEP,) + shape[1:], lambda i: (i,) + (0,) * (len(shape) - 1))

    layer = lambda a: pl.BlockSpec((1,) + a.shape[1:], lambda i: (0, 0, 0))
    tokens = bands_dev * frames
    return pl.pallas_call(
        functools.partial(time_kernel, len(kvs)),
        grid=(bands_dev // BSTEP,),
        in_specs=[band_block(q.shape), band_block(stream.shape)]
        + [band_block(a.shape) for a in kvs]
        + [layer(wo), layer(ff_in), layer(ff_out)],
        out_specs=band_block(stream.shape),
        out_shape=jax.ShapeDtypeStruct(stream.shape, BF),
        scratch_shapes=[
            pltpu.VMEM((BSTEP * frames, VW), BF),
            pltpu.VMEM((BSTEP * frames, ff), BF),
        ],
        cost_estimate=pl.CostEstimate(
            flops=4 * tokens * d * (ff + d), bytes_accessed=16 * tokens * d, transcendentals=0
        ),
        compiler_params=pltpu.CompilerParams(vmem_limit_bytes=32 << 20),
        name="time_layer",
    )(q, stream, *kvs, wo, ff_in, ff_out)


FSTEP = 8


def band_kernel(meta, table_ref, own_ref, far_ref, *refs):
    wq_ref, wkv_ref, wo_ref, w1_ref, w2_ref, out_ref, own32, far32, att_ref, hid_ref = refs
    bands, frames, d = own_ref.shape

    @pl.when(pl.program_id(0) == 0)
    def _():
        for source, wide in ((own_ref, own32), (far_ref, far32)):
            for j in range(d // LANES):
                part = source[:, :, j * LANES : (j + 1) * LANES].astype(F32)
                wide[j] = part.reshape(bands * frames, LANES)

    first_frame = pl.program_id(0) * FSTEP

    def rows(wide):
        parts = [
            jnp.concatenate(
                [wide[j, pl.ds(first_frame + f, bands, stride=frames), :] for f in range(FSTEP)], axis=0
            )
            for j in range(d // LANES)
        ]
        return jnp.concatenate(parts, axis=1)

    stream = rows(own32)
    n_own = rms(stream)
    n_far = rms(rows(far32))
    kv_own = mm(n_own, wkv_ref[0])
    kv_far = mm(n_far, wkv_ref[0])
    q = mm(n_own, wq_ref[0])
    t_own = table_ref[pl.ds(pl.multiple_of(meta[0] * bands, bands), bands), :]
    t_far = table_ref[pl.ds(pl.multiple_of((1 - meta[0]) * bands, bands), bands), :]
    t_q = t_own * (HEAD_DIM**-0.5 * math.log2(math.e))
    for c in range(CHUNKS):
        both = lambda x, t: jnp.concatenate(rotated(x, t, c), axis=1)
        k_own, k_far, q_c = both(kv_own, t_own), both(kv_far, t_far), both(q, t_q)
        lo = QW + c * PER * VPAD
        v_own = kv_own[:, lo : lo + PER * VPAD].astype(BF)
        v_far = kv_far[:, lo : lo + PER * VPAD].astype(BF)
        for f0 in range(0, FSTEP, BATCH):
            spans = [slice(f * bands, (f + 1) * bands) for f in range(f0, f0 + BATCH)]
            outs = attend(
                [q_c[at] for at in spans],
                [jnp.concatenate([k_own[at], k_far[at]], axis=0) for at in spans],
                [jnp.concatenate([v_own[at], v_far[at]], axis=0) for at in spans],
            )
            for at, out in zip(spans, outs):
                att_ref[at, c * PER * VPAD : (c + 1) * PER * VPAD] = out
    out = finish(stream, att_ref[...], wo_ref.at[0], w1_ref.at[0], w2_ref.at[0], hid_ref)
    out_ref[...] = out.astype(BF).reshape(out_ref.shape)


def band_layer(own, far, meta, table, wq, wkv, wo, ff_in, ff_out):
    bands, frames, d = own.shape
    ff = ff_in.shape[-1]
    whole = lambda a: pl.BlockSpec(a.shape, lambda i, *_: (0,) * len(a.shape))
    layer = lambda a: pl.BlockSpec((1,) + a.shape[1:], lambda i, *_: (1, 0, 0))
    tokens = bands * frames
    return pl.pallas_call(
        band_kernel,
        grid_spec=pltpu.PrefetchScalarGridSpec(
            num_scalar_prefetch=1,
            grid=(frames // FSTEP,),
            in_specs=[whole(table), whole(own), whole(far)]
            + [layer(a) for a in (wq, wkv, wo, ff_in, ff_out)],
            out_specs=pl.BlockSpec((FSTEP, bands, d), lambda i, *_: (i, 0, 0)),
            scratch_shapes=[
                pltpu.VMEM((d // LANES, bands * frames, LANES), F32),
                pltpu.VMEM((d // LANES, bands * frames, LANES), F32),
                pltpu.VMEM((bands * FSTEP, VW), BF),
                pltpu.VMEM((bands * FSTEP, ff), BF),
            ],
        ),
        out_shape=jax.ShapeDtypeStruct((frames, bands, d), BF),
        cost_estimate=pl.CostEstimate(
            flops=4 * tokens * d * (ff + 3 * d), bytes_accessed=16 * tokens * d, transcendentals=0
        ),
        compiler_params=pltpu.CompilerParams(vmem_limit_bytes=28 << 20),
        name="band_layer",
    )(meta, table, own, far, wq, wkv, wo, ff_in, ff_out)


def per_device(n, spectrogram, band_lengths, band_weight, attn_weights, ff_in, ff_out):
    frames, _, bins = spectrogram.shape
    bands_dev = band_weight.shape[0]
    order = list(range(0, n, 2)) + [i for i in range(n - 1, -1, -1) if i % 2]
    spot = {t: i for i, t in enumerate(order)}
    after = {t: order[(spot[t] + 1) % n] for t in order}
    before = {t: order[(spot[t] - 1) % n] for t in order}
    steps = n // 2
    book = np.zeros((n, 2, 2 + 2 * steps), np.int32)
    for t in range(n):
        for h in range(2):
            book[t, h, 0], book[t, h, 1] = h, t
            for s in range(1, steps + 1):
                sides = (order[(spot[t] - s) % n], order[(spot[t] + s) % n])
                book[t, h, 2 * s], book[t, h, 2 * s + 1] = sides[h], sides[1 - h]
    meta = lax.dynamic_slice(
        jnp.asarray(book),
        (lax.axis_index("tm"), lax.axis_index("head"), 0),
        (1, 1, book.shape[2]),
    ).reshape(-1)
    table = jnp.asarray(tables(n * frames))
    band_table = jnp.asarray(tables(2 * bands_dev))
    ring = [(2 * t, 2 * after[t]) for t in range(n)] + [
        (2 * t + 1, 2 * before[t] + 1) for t in range(n)
    ]
    swap = [(0, 1), (1, 0)]

    block = spectrogram.transpose(1, 0, 2).reshape(CH * frames, bins)
    near = lax.ppermute(block, ("tm", "head"), ring)
    wq, wkv, wo = prep(attn_weights)
    kv, q, stream = keys_values(
        [block], (1,), meta, band_lengths, table, band_weight, wkv, wq
    )
    near, kv = lax.optimization_barrier((near, kv))
    kvs, late = [kv], None
    for s in range(1, steps + 1):
        xs, slots = [near], [2 * s]
        if late is not None:
            xs.append(late)
            slots.append(2 * s - 1)
        if 2 * s != n:
            late = lax.ppermute(near, "head", swap)
        if s < steps:
            near = lax.ppermute(near, ("tm", "head"), ring)
        (kv,) = keys_values(xs, tuple(slots), meta, band_lengths, table, band_weight, wkv)
        near, late, kv = lax.optimization_barrier((near, late, kv))
        kvs.append(kv)
    if 2 * steps != n:
        kvs += keys_values(
            [late], (2 * steps + 1,), meta, band_lengths, table, band_weight, wkv
        )
    own = time_layer(q, stream, kvs, wo, ff_in, ff_out)
    far = lax.ppermute(own, "head", swap)
    return band_layer(own, far, meta, band_table, wq, wkv, wo, ff_in, ff_out)


def solution(mesh):
    return jax.shard_map(
        functools.partial(per_device, mesh.shape["tm"]),
        mesh=mesh,
        in_specs=(P(("groups", "tm"), None, None), P(), P("head", None, None), P(), P(), P()),
        out_specs=P(("groups", "tm"), "head", None),
        check_vma=False,
    )
```

```python
import functools
import math

import jax
import jax.numpy as jnp
import numpy as np
from jax import lax
from jax.experimental import pallas as pl
from jax.experimental.pallas import tpu as pltpu
from jax.sharding import PartitionSpec as P

HEADS = 8
HEAD_DIM = 48
MAXW = 32
CH = 4
HALF = HEAD_DIM // 2
HPAD = 32
VPAD = 64
LANES = 128
PER = LANES // HPAD
CHUNKS = HEADS // PER
QW = 2 * HEADS * HPAD
VW = HEADS * VPAD
GROUP = LANES // MAXW
CW = 2 * LANES
BSTEP = 8
BATCH = 8
BF = jnp.bfloat16
F32 = jnp.float32


ONCHIP = pl.BlockSpec(memory_space=pltpu.VMEM)
KV_BYTES = 20 << 20


def mm(a, b):
    return jnp.dot(a, b, preferred_element_type=F32)


def mm_nt(a, b):
    return lax.dot_general(a, b, (((1,), (1,)), ((), ())), preferred_element_type=F32)


def rms(x):
    return (x * lax.rsqrt(jnp.mean(x * x, axis=-1, keepdims=True) + 1e-06)).astype(BF)


def tables(count):
    freq = 10000.0 ** (-np.arange(HALF, dtype=np.float64) / HALF)
    angle = np.arange(count, dtype=np.float64)[:, None] * freq
    pad = ((0, 0), (0, HPAD - HALF))
    cosine = np.tile(np.pad(np.cos(angle), pad), (1, PER))
    sine = np.tile(np.pad(np.sin(angle), pad), (1, PER))
    return np.concatenate([cosine, sine], axis=1).astype(np.float32)


def rotated(x, table, c):
    period = table.shape[0]
    u = x[:, c * CW : c * CW + LANES].reshape(-1, period, LANES)
    w = x[:, c * CW + LANES : (c + 1) * CW].reshape(-1, period, LANES)
    cosine, sine = table[None, :, :LANES], table[None, :, LANES:]
    first = (u * cosine - w * sine).reshape(-1, LANES)
    second = (w * cosine + u * sine).reshape(-1, LANES)
    return jnp.concatenate([first, second], axis=1)


def gelu(x):
    return 0.5 * x * (1.0 + lax.erf(x * math.sqrt(0.5)))


def finish(stream, att, wo, w1, w2, hid_ref):
    mid = stream + mm(att, wo[...])
    normed = rms(mid)
    width = w1.shape[-1]
    step = 256
    for j in range(0, width, step):
        hid_ref[:, j : j + step] = gelu(mm(normed, w1[:, j : j + step])).astype(BF)
    return mid + mm(hid_ref[...], w2[...])


def attend(queries, keys, values):
    m = queries[0].shape[0]
    own = (lax.broadcasted_iota(jnp.int32, (1, CW), 1) % LANES) // HPAD
    vlane = lax.broadcasted_iota(jnp.int32, (1, PER * VPAD), 1) // VPAD
    stacked = [
        jnp.concatenate([jnp.where(own == h, q, jnp.zeros_like(q)) for h in range(PER)], axis=0)
        for q in queries
    ]
    scores = [mm_nt(q, k) for q, k in zip(stacked, keys)]
    highest = [jnp.max(s, axis=-1, keepdims=True) for s in scores]
    powers = [jnp.exp2(s - h) for s, h in zip(scores, highest)]
    sums = [jnp.sum(p, axis=-1, keepdims=True) for p in powers]
    mixed = [mm(p.astype(BF), v) for p, v in zip(powers, values)]
    outs = []
    for r, total in zip(mixed, sums):
        r = r * (1.0 / total)
        out = r[:m]
        for h in range(1, PER):
            out = jnp.where(vlane == h, r[h * m : (h + 1) * m], out)
        outs.append(out.astype(BF))
    return outs


def prep_kernel(lens_ref, w_ref, wq_ref, wkv_ref, wo_ref, starts_ref, held_ref, sem):
    layers, kinds, d, _ = w_ref.shape
    copies = [
        [pltpu.make_async_copy(w_ref.at[i, j], held_ref.at[i, j], sem.at[i, j]) for j in range(kinds)]
        for i in range(layers)
    ]
    for layer in copies:
        for copy in layer:
            copy.start()
    start = jnp.int32(0)
    for b in range(lens_ref.shape[0]):
        starts_ref[b] = start
        start = start + lens_ref[b]
    row = lax.broadcasted_iota(jnp.int32, (d, QW), 0)
    col = lax.broadcasted_iota(jnp.int32, (d, QW), 1)
    inner = col % HPAD
    head = (col // CW) * PER + (col % LANES) // HPAD
    source = head * HEAD_DIM + ((col % CW) // LANES) * HALF + inner
    pick = jnp.where((row == source) & (inner < HALF), 1.0, 0.0).astype(BF)
    vcol = lax.broadcasted_iota(jnp.int32, (d, VW), 1)
    vrow = lax.broadcasted_iota(jnp.int32, (d, VW), 0)
    vpick = jnp.where(
        (vrow == (vcol // VPAD) * HEAD_DIM + vcol % VPAD) & (vcol % VPAD < HEAD_DIM), 1.0, 0.0
    ).astype(BF)
    orow = lax.broadcasted_iota(jnp.int32, (VW, d), 0)
    ocol = lax.broadcasted_iota(jnp.int32, (VW, d), 1)
    opick = jnp.where(
        (ocol == (orow // VPAD) * HEAD_DIM + orow % VPAD) & (orow % VPAD < HEAD_DIM), 1.0, 0.0
    ).astype(BF)
    for i in range(layers):
        for copy in copies[i]:
            copy.wait()
        wq_ref[i] = mm(held_ref[i, 0], pick).astype(BF)
        wkv_ref[i, :, :QW] = mm(held_ref[i, 1], pick).astype(BF)
        wkv_ref[i, :, QW:] = mm(held_ref[i, 2], vpick).astype(BF)
        wo_ref[i] = mm(opick, held_ref[i, 3]).astype(BF)


def prep(attn_weights, band_lengths):
    layers, kinds, d, _ = attn_weights.shape
    return pl.pallas_call(
        prep_kernel,
        in_specs=[
            pl.BlockSpec(memory_space=pltpu.SMEM),
            pl.BlockSpec(memory_space=pltpu.HBM),
        ],
        out_specs=[ONCHIP] * 3 + [pl.BlockSpec(memory_space=pltpu.SMEM)],
        out_shape=[
            jax.ShapeDtypeStruct((layers, d, QW), BF),
            jax.ShapeDtypeStruct((layers, d, QW + VW), BF),
            jax.ShapeDtypeStruct((layers, VW, d), BF),
            jax.ShapeDtypeStruct(band_lengths.shape, jnp.int32),
        ],
        scratch_shapes=[
            pltpu.VMEM(attn_weights.shape, BF),
            pltpu.SemaphoreType.DMA((layers, kinds)),
        ],
        cost_estimate=pl.CostEstimate(
            flops=layers * 8 * d * d * QW, bytes_accessed=layers * 16 * d * d, transcendentals=0
        ),
        compiler_params=pltpu.CompilerParams(vmem_limit_bytes=24 << 20),
        name="prep",
    )(band_lengths, attn_weights)


def embed(x_refs, weight_ref, band0, lens, starts):
    rows, bins = x_refs[0].shape
    frames = rows // CH
    lane = lax.broadcasted_iota(jnp.int32, (1, LANES), 1)
    inner = lane % MAXW
    bin_row = lax.broadcasted_iota(jnp.int32, (2 * LANES, LANES), 0)
    groups = [range(b, b + GROUP) for b in range(0, BSTEP, GROUP)]
    picked = []
    for ids in groups:
        base = jnp.minimum(starts[ids[0]] // LANES, (bins - 2 * LANES) // LANES) * LANES
        base = pl.multiple_of(base, LANES)
        target = jnp.full((1, LANES), -1, jnp.int32)
        for k, b in enumerate(ids):
            mine = (lane // MAXW == k) & (inner < lens[b])
            target = jnp.where(mine, starts[b] - base + inner, target)
        select = jnp.where(bin_row == target, 1.0, 0.0).astype(BF)
        window = jnp.concatenate([x[:, pl.ds(base, 2 * LANES)] for x in x_refs], axis=0)
        picked.append(mm(window, select))
    scales, lefts = [], []
    for ids, features in zip(groups, picked):
        narrow = features.astype(BF)
        square = features * features
        scale, left = [], []
        for i in range(len(x_refs)):
            spots = [slice(i * rows + c * frames, i * rows + (c + 1) * frames) for c in range(CH)]
            total = square[spots[0]]
            for spot in spots[1:]:
                total = total + square[spot]
            for k, b in enumerate(ids):
                mine = lane // MAXW == k
                mean = jnp.sum(jnp.where(mine, total, 0.0), axis=-1, keepdims=True) / (
                    (CH * lens[b]).astype(F32)
                )
                scale.append(lax.rsqrt(jnp.maximum(mean, 0.25)))
                kept = [jnp.where(mine, narrow[spot], jnp.zeros((), BF)) for spot in spots]
                left.append(jnp.concatenate(kept, axis=1))
        scales.append(jnp.concatenate(scale, axis=0))
        lefts.append(jnp.concatenate(left, axis=0))
    streams = []
    for ids, left, scale in zip(groups, lefts, scales):
        weight = jnp.concatenate(
            [weight_ref[band0 + b, c * MAXW : (c + 1) * MAXW, :] for c in range(CH) for b in ids],
            axis=0,
        )
        streams.append(mm(left, weight) * scale)
    return jnp.concatenate(streams, axis=0)


def source_block(n, step, side):
    t, h = lax.axis_index("tm"), lax.axis_index("head")
    spot = jnp.where(t % 2 == 0, t // 2, n - 1 - t // 2)
    back = (h == 0) == (side == 0)
    spot = lax.rem(jnp.where(back, spot - step, spot + step) + n, n)
    return jnp.where(spot < (n + 1) // 2, 2 * spot, 2 * (n - 1 - spot) + 1)


def kv_kernel(n, blocks, slots, with_q, resident, lens_ref, starts_ref, table_ref, *refs):
    x_refs, refs = refs[:blocks], refs[blocks:]
    weight_ref, wkv_ref, *refs = refs
    if with_q:
        wq_ref, *refs = refs
    kv_ref = refs[0]
    bands_dev = weight_ref.shape[0]
    frames = x_refs[0].shape[0] // CH
    band0 = pl.program_id(0) * BSTEP
    first = lax.axis_index("head") * bands_dev + band0
    lens = [lens_ref[first + b] for b in range(BSTEP)]
    starts = [starts_ref[first + b] for b in range(BSTEP)]
    stream = embed(x_refs, weight_ref, band0, lens, starts)
    normed = rms(stream)
    kv = mm(normed, wkv_ref[0])
    places = [pl.multiple_of(source_block(n, *slot) * frames, frames) for slot in slots]
    table = jnp.concatenate(
        [table_ref[pl.ds(p, frames), :] for p in places for _ in range(GROUP)], axis=0
    )

    def put(ref, base, cols, value):
        width = value.shape[1]
        value = value.reshape(BSTEP // GROUP, blocks, GROUP, frames, width)
        for g in range(BSTEP // GROUP):
            bands = pl.ds(base + g * GROUP, GROUP)
            if len(ref.shape) == 3:
                ref[bands, :, cols : cols + width] = value[g, 0]
                continue
            for i in range(blocks):
                ref[bands, i, :, cols : cols + width] = value[g, i]

    base = band0 if resident else 0
    for c in range(CHUNKS):
        put(kv_ref, base, c * CW, rotated(kv, table, c).astype(BF))
    put(kv_ref, base, QW, kv[:, QW:].astype(BF))
    if with_q:
        q_ref, stream_ref = refs[1:]
        q = mm(normed, wq_ref[0])
        scaled = table * (HEAD_DIM**-0.5 * math.log2(math.e))
        for c in range(CHUNKS):
            put(q_ref, band0, c * CW, rotated(q, scaled, c).astype(BF))
        put(stream_ref, band0, 0, stream.astype(BF))


def keys_values(n, xs, slots, resident, lens, starts, table, band_weight, wkv, wq=None):
    blocks = len(xs)
    with_q = wq is not None
    rows, bins = xs[0].shape
    frames = rows // CH
    bands_dev, feat, d = band_weight.shape
    kvw = QW + VW
    lead = () if blocks == 1 else (blocks,)
    zeros = (0,) * (len(lead) + 2)
    out_shape = [jax.ShapeDtypeStruct((bands_dev,) + lead + (frames, kvw), BF)]
    out_specs = [
        ONCHIP
        if resident
        else pl.BlockSpec((BSTEP,) + lead + (frames, kvw), lambda i, *_: (i,) + zeros)
    ]
    args = [table, *xs, band_weight, wkv]
    if with_q:
        args.append(wq)
        for width in (QW, d):
            out_shape.append(jax.ShapeDtypeStruct((bands_dev, frames, width), BF))
            out_specs.append(ONCHIP)
    tokens = blocks * frames * bands_dev
    return pl.pallas_call(
        functools.partial(kv_kernel, n, blocks, slots, with_q, resident),
        grid_spec=pltpu.PrefetchScalarGridSpec(
            num_scalar_prefetch=2,
            grid=(bands_dev // BSTEP,),
            in_specs=[ONCHIP] * len(args),
            out_specs=out_specs,
        ),
        out_shape=out_shape,
        cost_estimate=pl.CostEstimate(
            flops=2 * tokens * d * (kvw + 4 * feat),
            bytes_accessed=2 * (tokens * kvw + d * kvw + bands_dev * feat * d),
            transcendentals=0,
        ),
        compiler_params=pltpu.CompilerParams(vmem_limit_bytes=24 << 20),
        name="keys_values",
    )(lens, starts, *args)


def time_kernel(parts, resident, q_ref, stream_ref, *refs):
    kv_refs, refs = refs[:parts], refs[parts:]
    wo_ref, w1_ref, w2_ref, out_ref, normed_ref, att_ref, hid_ref = refs
    frames = q_ref.shape[1]
    d = stream_ref.shape[-1]
    band0 = pl.program_id(0) * BSTEP
    kv0 = band0 if resident else 0
    for c in range(CHUNKS):
        lo = QW + c * PER * VPAD

        def keyed(b, start, width):
            parts = [r[kv0 + b, ..., start : start + width].reshape(-1, width) for r in kv_refs]
            return jnp.concatenate(parts, axis=0)

        for b0 in range(0, BSTEP, BATCH):
            ids = range(b0, b0 + BATCH)
            outs = attend(
                [q_ref[band0 + b, :, c * CW : (c + 1) * CW] for b in ids],
                [keyed(b, c * CW, CW) for b in ids],
                [keyed(b, lo, PER * VPAD) for b in ids],
            )
            for b, out in zip(ids, outs):
                att_ref[b * frames : (b + 1) * frames, c * PER * VPAD : (c + 1) * PER * VPAD] = out
    stream = stream_ref[pl.ds(band0, BSTEP)].reshape(BSTEP * frames, d).astype(F32)
    out = finish(stream, att_ref[...], wo_ref.at[0], w1_ref.at[0], w2_ref.at[0], hid_ref)
    rows = BSTEP * frames
    row = lax.broadcasted_iota(jnp.int32, (rows, rows), 0)
    col = lax.broadcasted_iota(jnp.int32, (rows, rows), 1)
    turn = jnp.where(col == (row % BSTEP) * frames + row // BSTEP, 1.0, 0.0).astype(BF)
    turned = mm(turn, out.astype(BF))
    out_ref[pl.program_id(0)] = turned.astype(BF)
    normed_ref[pl.program_id(0)] = rms(turned)


def time_layer(q, stream, kvs, resident, wo, ff_in, ff_out):
    bands_dev, frames, d = stream.shape
    ff = ff_in.shape[-1]

    def kv_spec(a):
        if resident:
            return ONCHIP
        return pl.BlockSpec((BSTEP,) + a.shape[1:], lambda i: (i,) + (0,) * (len(a.shape) - 1))

    tokens = bands_dev * frames
    out_shape = jax.ShapeDtypeStruct((bands_dev // BSTEP, frames * BSTEP, d), BF)
    return pl.pallas_call(
        functools.partial(time_kernel, len(kvs), resident),
        grid=(bands_dev // BSTEP,),
        in_specs=[ONCHIP] * 2 + [kv_spec(a) for a in kvs] + [ONCHIP] * 3,
        out_specs=[ONCHIP] * 2,
        out_shape=[out_shape] * 2,
        scratch_shapes=[
            pltpu.VMEM((BSTEP * frames, VW), BF),
            pltpu.VMEM((BSTEP * frames, ff), BF),
        ],
        cost_estimate=pl.CostEstimate(
            flops=4 * tokens * d * (ff + d), bytes_accessed=16 * tokens * d, transcendentals=0
        ),
        compiler_params=pltpu.CompilerParams(vmem_limit_bytes=(16 if resident else 56) << 20),
        name="time_layer",
    )(q, stream, *kvs, wo, ff_in, ff_out)


FSTEP = 8


def band_table(table_ref, which, parts):
    bands = parts * BSTEP
    t = table_ref[pl.ds(pl.multiple_of(which * bands, bands), bands), :]
    t = t.reshape(parts, 1, BSTEP, 2 * LANES)
    return jnp.broadcast_to(t, (parts, FSTEP, BSTEP, 2 * LANES)).reshape(-1, 2 * LANES)


def frame_rows(x, f, parts):
    step = x.shape[0] // parts
    pieces = [x[p * step + f * BSTEP : p * step + (f + 1) * BSTEP] for p in range(parts)]
    return jnp.concatenate(pieces, axis=0)


def own_kernel(table_ref, own_ref, wq_ref, wkv_ref, out_ref):
    parts, _, d = own_ref.shape
    rows = FSTEP * BSTEP
    here = pl.ds(pl.multiple_of(pl.program_id(0) * rows, rows), rows)
    n_own = own_ref[:, here, :].reshape(parts * rows, d)
    kv = mm(n_own, wkv_ref[1])
    q = mm(n_own, wq_ref[1])
    table = band_table(table_ref, lax.axis_index("head"), parts)
    scaled = table * (HEAD_DIM**-0.5 * math.log2(math.e))
    values = [rotated(q, scaled, c) for c in range(CHUNKS)]
    values += [rotated(kv, table, c) for c in range(CHUNKS)] + [kv[:, QW:]]
    at = 0
    for value in values:
        width = value.shape[1]
        for f in range(FSTEP):
            frame = pl.program_id(0) * FSTEP + f
            out_ref[frame, :, at : at + width] = frame_rows(value, f, parts).astype(BF)
        at += width


def own_projections(own, table, wq, wkv):
    parts, rows, d = own.shape
    frames, bands = rows // BSTEP, parts * BSTEP
    width = 2 * QW + VW
    return pl.pallas_call(
        own_kernel,
        grid=(frames // FSTEP,),
        in_specs=[ONCHIP] * 4,
        out_specs=ONCHIP,
        out_shape=jax.ShapeDtypeStruct((frames, bands, width), BF),
        cost_estimate=pl.CostEstimate(
            flops=2 * frames * bands * d * width,
            bytes_accessed=4 * frames * bands * width,
            transcendentals=0,
        ),
        compiler_params=pltpu.CompilerParams(vmem_limit_bytes=16 << 20),
        name="own_projections",
    )(table, own, wq, wkv)


def band_kernel(table_ref, stream_ref, own_ref, far_ref, *refs):
    wkv_ref, wo_ref, w1_ref, w2_ref, out_ref, att_ref, hid_ref = refs
    parts, _, d = stream_ref.shape
    bands = parts * BSTEP
    rows = FSTEP * BSTEP
    here = pl.ds(pl.multiple_of(pl.program_id(0) * rows, rows), rows)
    first = pl.program_id(0) * FSTEP
    kv = mm(far_ref[:, here, :].reshape(parts * rows, d), wkv_ref[1])
    table = band_table(table_ref, 1 - lax.axis_index("head"), parts)
    for c in range(CHUNKS):
        keys = rotated(kv, table, c)
        lo, wide = QW + c * PER * VPAD, PER * VPAD
        values = kv[:, lo : lo + wide]

        def joined(x, f, start):
            ours = own_ref[first + f, :, start : start + x.shape[1]]
            return jnp.concatenate([ours, frame_rows(x, f, parts).astype(BF)], axis=0)

        for f0 in range(0, FSTEP, BATCH):
            ids = range(f0, f0 + BATCH)
            outs = attend(
                [own_ref[first + f, :, c * CW : (c + 1) * CW] for f in ids],
                [joined(keys, f, QW + c * CW) for f in ids],
                [joined(values, f, QW + lo) for f in ids],
            )
            for f, out in zip(ids, outs):
                att_ref[f * bands : (f + 1) * bands, c * wide : (c + 1) * wide] = out
    stream = stream_ref[:, here, :].reshape(parts * rows, d).astype(F32)
    stream = jnp.concatenate([frame_rows(stream, f, parts) for f in range(FSTEP)], axis=0)
    out = finish(stream, att_ref[...], wo_ref.at[1], w1_ref.at[1], w2_ref.at[1], hid_ref)
    out_ref[...] = out.astype(BF).reshape(out_ref.shape)


def band_layer(stream, own, far, table, wkv, wo, ff_in, ff_out):
    parts, rows, d = stream.shape
    frames, bands = rows // BSTEP, parts * BSTEP
    ff = ff_in.shape[-1]
    tokens = bands * frames
    return pl.pallas_call(
        band_kernel,
        grid=(frames // FSTEP,),
        in_specs=[ONCHIP] * 8,
        out_specs=pl.BlockSpec((FSTEP, bands, d), lambda i: (i, 0, 0)),
        scratch_shapes=[
            pltpu.VMEM((bands * FSTEP, VW), BF),
            pltpu.VMEM((bands * FSTEP, ff), BF),
        ],
        out_shape=jax.ShapeDtypeStruct((frames, bands, d), BF),
        cost_estimate=pl.CostEstimate(
            flops=4 * tokens * d * (ff + 3 * d), bytes_accessed=16 * tokens * d, transcendentals=0
        ),
        compiler_params=pltpu.CompilerParams(vmem_limit_bytes=28 << 20),
        name="band_layer",
    )(table, stream, own, far, wkv, wo, ff_in, ff_out)


def per_device(n, spectrogram, band_lengths, band_weight, attn_weights, ff_in, ff_out):
    frames, _, bins = spectrogram.shape
    bands_dev = band_weight.shape[0]
    order = list(range(0, n, 2)) + [i for i in range(n - 1, -1, -1) if i % 2]
    spot = {t: i for i, t in enumerate(order)}
    after = {t: order[(spot[t] + 1) % n] for t in order}
    before = {t: order[(spot[t] - 1) % n] for t in order}
    steps = n // 2
    resident = 2 * bands_dev * n * frames * (QW + VW) <= KV_BYTES
    table = jnp.asarray(tables(n * frames))
    positions = jnp.asarray(tables(2 * bands_dev))
    ring = [(2 * t, 2 * after[t]) for t in range(n)] + [
        (2 * t + 1, 2 * before[t] + 1) for t in range(n)
    ]
    swap = [(0, 1), (1, 0)]

    block = spectrogram.transpose(1, 0, 2).reshape(CH * frames, bins)
    near = lax.ppermute(block, ("tm", "head"), ring)
    wq, wkv, wo, starts = prep(attn_weights, band_lengths)
    project = functools.partial(keys_values, n)
    weights = (resident, band_lengths, starts, table, band_weight, wkv)
    kv, q, stream = project([block], ((0, 0),), *weights, wq)
    near, kv = lax.optimization_barrier((near, kv))
    kvs, late = [kv], None
    for s in range(1, steps + 1):
        xs, slots = [near], [(s, 0)]
        if late is not None:
            xs.append(late)
            slots.append((s - 1, 1))
        if 2 * s != n:
            late = lax.ppermute(near, "head", swap)
        if s < steps:
            near = lax.ppermute(near, ("tm", "head"), ring)
        (kv,) = project(xs, tuple(slots), *weights)
        near, late, kv = lax.optimization_barrier((near, late, kv))
        kvs.append(kv)
    if 2 * steps != n:
        kvs += project([late], ((steps, 1),), *weights)
    stream, own = time_layer(q, stream, kvs, resident, wo, ff_in, ff_out)
    far = lax.ppermute(own, "head", swap)
    own = own_projections(own, positions, wq, wkv)
    return band_layer(stream, own, far, positions, wkv, wo, ff_in, ff_out)


def solution(mesh):
    return jax.shard_map(
        functools.partial(per_device, mesh.shape["tm"]),
        mesh=mesh,
        in_specs=(P(("groups", "tm"), None, None), P(), P("head", None, None), P(), P(), P()),
        out_specs=P(("groups", "tm"), "head", None),
        check_vma=False,
    )
```

```python
import functools
import math

import jax
import jax.numpy as jnp
import numpy as np
from jax import lax
from jax.experimental import pallas as pl
from jax.experimental.pallas import tpu as pltpu
from jax.sharding import PartitionSpec as P

HEADS = 8
HEAD_DIM = 48
MAXW = 32
CH = 4
HALF = HEAD_DIM // 2
HPAD = 32
VPAD = 64
LANES = 128
PER = LANES // HPAD
CHUNKS = HEADS // PER
QW = 2 * HEADS * HPAD
VW = HEADS * VPAD
GROUP = LANES // MAXW
CW = 2 * LANES
BSTEP = 8
KSTEP = 16
TPARTS = 2
BATCH = 8
BF = jnp.bfloat16
F32 = jnp.float32


ONCHIP = pl.BlockSpec(memory_space=pltpu.VMEM)
KV_BYTES = 20 << 20


def mm(a, b):
    return jnp.dot(a, b, preferred_element_type=F32)


def mm_nt(a, b):
    return lax.dot_general(a, b, (((1,), (1,)), ((), ())), preferred_element_type=F32)


def rms(x):
    return (x * lax.rsqrt(jnp.mean(x * x, axis=-1, keepdims=True) + 1e-06)).astype(BF)


def tables(count):
    freq = 10000.0 ** (-np.arange(HALF, dtype=np.float64) / HALF)
    angle = np.arange(count, dtype=np.float64)[:, None] * freq
    pad = ((0, 0), (0, HPAD - HALF))
    cosine = np.tile(np.pad(np.cos(angle), pad), (1, PER))
    sine = np.tile(np.pad(np.sin(angle), pad), (1, PER))
    return np.concatenate([cosine, sine], axis=1).astype(np.float32)


def rotated(x, table, c):
    period = table.shape[0]
    u = x[:, c * CW : c * CW + LANES].reshape(-1, period, LANES)
    w = x[:, c * CW + LANES : (c + 1) * CW].reshape(-1, period, LANES)
    cosine, sine = table[None, :, :LANES], table[None, :, LANES:]
    first = (u * cosine - w * sine).reshape(-1, LANES)
    second = (w * cosine + u * sine).reshape(-1, LANES)
    return jnp.concatenate([first, second], axis=1)


def gelu(x):
    return 0.5 * x * (1.0 + lax.erf(x * math.sqrt(0.5)))


def finish(stream, att, wo, w1, w2, hid_ref):
    mid = stream + mm(att, wo[...])
    normed = rms(mid)
    width = w1.shape[-1]
    step = 256
    for j in range(0, width, step):
        hid_ref[:, j : j + step] = gelu(mm(normed, w1[:, j : j + step])).astype(BF)
    return mid + mm(hid_ref[...], w2[...])


def attend(queries, keys, values):
    m = queries[0].shape[0]
    own = (lax.broadcasted_iota(jnp.int32, (1, CW), 1) % LANES) // HPAD
    vlane = lax.broadcasted_iota(jnp.int32, (1, PER * VPAD), 1) // VPAD
    stacked = [
        jnp.concatenate([jnp.where(own == h, q, jnp.zeros_like(q)) for h in range(PER)], axis=0)
        for q in queries
    ]
    scores = [mm_nt(q, k) for q, k in zip(stacked, keys)]
    highest = [jnp.max(s, axis=-1, keepdims=True) for s in scores]
    powers = [jnp.exp2(s - h) for s, h in zip(scores, highest)]
    sums = [jnp.sum(p, axis=-1, keepdims=True) for p in powers]
    mixed = [mm(p.astype(BF), v) for p, v in zip(powers, values)]
    outs = []
    for r, total in zip(mixed, sums):
        r = r * (1.0 / total)
        out = r[:m]
        for h in range(1, PER):
            out = jnp.where(vlane == h, r[h * m : (h + 1) * m], out)
        outs.append(out.astype(BF))
    return outs


def prep_kernel(w_ref, wq_ref, wkv_ref, wo_ref):
    layers, _, d, _ = w_ref.shape
    share = d // CHUNKS
    span = -(-share // LANES) * LANES
    for c in range(CHUNKS):
        low = min(c * share // LANES * LANES, d - span)
        shift = c * share - low
        row = lax.broadcasted_iota(jnp.int32, (span, CW), 0)
        col = lax.broadcasted_iota(jnp.int32, (span, CW), 1)
        inner = col % HPAD
        source = (col % LANES) // HPAD * HEAD_DIM + col // LANES * HALF + inner + shift
        pick = jnp.where((row == source) & (inner < HALF), 1.0, 0.0).astype(BF)
        inner = col % VPAD
        source = col // VPAD * HEAD_DIM + inner + shift
        vpick = jnp.where((row == source) & (inner < HEAD_DIM), 1.0, 0.0).astype(BF)
        row = lax.broadcasted_iota(jnp.int32, (CW, span), 0)
        col = lax.broadcasted_iota(jnp.int32, (CW, span), 1)
        inner = row % VPAD
        source = row // VPAD * HEAD_DIM + inner + shift
        opick = jnp.where((col == source) & (inner < HEAD_DIM), 1.0, 0.0).astype(BF)
        to = slice(c * CW, (c + 1) * CW)
        for i in range(layers):
            part = slice(low, low + span)
            wq_ref[i, :, to] = mm(w_ref[i, 0, :, part], pick).astype(BF)
            wkv_ref[i, :, to] = mm(w_ref[i, 1, :, part], pick).astype(BF)
            at = slice(QW + c * CW, QW + (c + 1) * CW)
            wkv_ref[i, :, at] = mm(w_ref[i, 2, :, part], vpick).astype(BF)
            wo_ref[i, to, :] = mm(opick, w_ref[i, 3, part, :]).astype(BF)


def prep(attn_weights):
    layers, _, d, _ = attn_weights.shape
    return pl.pallas_call(
        prep_kernel,
        in_specs=[ONCHIP],
        out_specs=[ONCHIP] * 3,
        out_shape=[
            jax.ShapeDtypeStruct((layers, d, QW), BF),
            jax.ShapeDtypeStruct((layers, d, QW + VW), BF),
            jax.ShapeDtypeStruct((layers, VW, d), BF),
        ],
        cost_estimate=pl.CostEstimate(
            flops=layers * 8 * d * d * QW, bytes_accessed=layers * 16 * d * d, transcendentals=0
        ),
        compiler_params=pltpu.CompilerParams(vmem_limit_bytes=16 << 20),
        name="prep",
    )(attn_weights)


def embed(x_refs, weight_ref, band0, lens, starts):
    rows, bins = x_refs[0].shape
    frames = rows // CH
    lane = lax.broadcasted_iota(jnp.int32, (1, LANES), 1)
    inner = lane % MAXW
    bin_row = lax.broadcasted_iota(jnp.int32, (2 * LANES, LANES), 0)
    groups = [range(b, b + GROUP) for b in range(0, KSTEP, GROUP)]
    picked = []
    for ids in groups:
        base = jnp.minimum(starts[ids[0]] // LANES, (bins - 2 * LANES) // LANES) * LANES
        base = pl.multiple_of(base, LANES)
        target = jnp.full((1, LANES), -1, jnp.int32)
        for k, b in enumerate(ids):
            mine = (lane // MAXW == k) & (inner < lens[b])
            target = jnp.where(mine, starts[b] - base + inner, target)
        select = jnp.where(bin_row == target, 1.0, 0.0).astype(BF)
        window = jnp.concatenate([x[:, pl.ds(base, 2 * LANES)] for x in x_refs], axis=0)
        picked.append(mm(window, select))
    scales, lefts = [], []
    for ids, features in zip(groups, picked):
        narrow = features.astype(BF)
        square = features * features
        scale, left = [], []
        for i in range(len(x_refs)):
            spots = [slice(i * rows + c * frames, i * rows + (c + 1) * frames) for c in range(CH)]
            total = square[spots[0]]
            for spot in spots[1:]:
                total = total + square[spot]
            for k, b in enumerate(ids):
                mine = lane // MAXW == k
                mean = jnp.sum(jnp.where(mine, total, 0.0), axis=-1, keepdims=True) / (
                    (CH * lens[b]).astype(F32)
                )
                scale.append(lax.rsqrt(jnp.maximum(mean, 0.25)))
                kept = [jnp.where(mine, narrow[spot], jnp.zeros((), BF)) for spot in spots]
                left.append(jnp.concatenate(kept, axis=1))
        scales.append(jnp.concatenate(scale, axis=0))
        lefts.append(jnp.concatenate(left, axis=0))
    streams = []
    for ids, left, scale in zip(groups, lefts, scales):
        weight = jnp.concatenate(
            [weight_ref[band0 + b, c * MAXW : (c + 1) * MAXW, :] for c in range(CH) for b in ids],
            axis=0,
        )
        streams.append(mm(left, weight) * scale)
    return jnp.concatenate(streams, axis=0)


def source_block(n, step, side):
    t, h = lax.axis_index("tm"), lax.axis_index("head")
    spot = jnp.where(t % 2 == 0, t // 2, n - 1 - t // 2)
    back = (h == 0) == (side == 0)
    spot = lax.rem(jnp.where(back, spot - step, spot + step) + n, n)
    return jnp.where(spot < (n + 1) // 2, 2 * spot, 2 * (n - 1 - spot) + 1)


def kv_kernel(n, blocks, slots, with_q, resident, lens_ref, *refs):
    if with_q:
        *refs, starts_ref = refs

        @pl.when(pl.program_id(0) == 0)
        def _():
            start = jnp.int32(0)
            for b in range(lens_ref.shape[0]):
                starts_ref[b] = start
                start = start + lens_ref[b]

    else:
        starts_ref, *refs = refs
    table_ref, *refs = refs
    x_refs, refs = refs[:blocks], refs[blocks:]
    weight_ref, wkv_ref, *refs = refs
    if with_q:
        wq_ref, *refs = refs
    kv_ref = refs[0]
    bands_dev = weight_ref.shape[0]
    frames = x_refs[0].shape[0] // CH
    band0 = pl.program_id(0) * KSTEP
    first = lax.axis_index("head") * bands_dev + band0
    lens = [lens_ref[first + b] for b in range(KSTEP)]
    starts = [starts_ref[first + b] for b in range(KSTEP)]
    stream = embed(x_refs, weight_ref, band0, lens, starts)
    normed = rms(stream)
    kv = mm(normed, wkv_ref[0])
    places = [pl.multiple_of(source_block(n, *slot) * frames, frames) for slot in slots]
    table = jnp.concatenate(
        [table_ref[pl.ds(p, frames), :] for p in places for _ in range(GROUP)], axis=0
    )

    def put(ref, base, cols, value):
        width = value.shape[1]
        value = value.reshape(KSTEP // GROUP, blocks, GROUP, frames, width)
        for g in range(KSTEP // GROUP):
            bands = pl.ds(base + g * GROUP, GROUP)
            if len(ref.shape) == 3:
                ref[bands, :, cols : cols + width] = value[g, 0]
                continue
            for i in range(blocks):
                ref[bands, i, :, cols : cols + width] = value[g, i]

    base = band0 if resident else 0
    for c in range(CHUNKS):
        put(kv_ref, base, c * CW, rotated(kv, table, c).astype(BF))
    put(kv_ref, base, QW, kv[:, QW:].astype(BF))
    if with_q:
        q_ref, stream_ref = refs[1:3]
        q = mm(normed, wq_ref[0])
        scaled = table * (HEAD_DIM**-0.5 * math.log2(math.e))
        for c in range(CHUNKS):
            put(q_ref, band0, c * CW, rotated(q, scaled, c).astype(BF))
        put(stream_ref, band0, 0, stream.astype(BF))


def keys_values(n, xs, slots, resident, lens, table, band_weight, wkv, starts=None, wq=None):
    blocks = len(xs)
    with_q = wq is not None
    rows, bins = xs[0].shape
    frames = rows // CH
    bands_dev, feat, d = band_weight.shape
    kvw = QW + VW
    lead = () if blocks == 1 else (blocks,)
    zeros = (0,) * (len(lead) + 2)
    out_shape = [jax.ShapeDtypeStruct((bands_dev,) + lead + (frames, kvw), BF)]
    out_specs = [
        ONCHIP
        if resident
        else pl.BlockSpec((KSTEP,) + lead + (frames, kvw), lambda i, *_: (i,) + zeros)
    ]
    args = [table, *xs, band_weight, wkv]
    if with_q:
        args.append(wq)
        for width in (QW, d):
            out_shape.append(jax.ShapeDtypeStruct((bands_dev, frames, width), BF))
            out_specs.append(ONCHIP)
        out_shape.append(jax.ShapeDtypeStruct(lens.shape, jnp.int32))
        out_specs.append(pl.BlockSpec(memory_space=pltpu.SMEM))
    scalars = [lens] if with_q else [lens, starts]
    tokens = blocks * frames * bands_dev
    return pl.pallas_call(
        functools.partial(kv_kernel, n, blocks, slots, with_q, resident),
        grid_spec=pltpu.PrefetchScalarGridSpec(
            num_scalar_prefetch=len(scalars),
            grid=(bands_dev // KSTEP,),
            in_specs=[ONCHIP] * len(args),
            out_specs=out_specs,
        ),
        out_shape=out_shape,
        cost_estimate=pl.CostEstimate(
            flops=2 * tokens * d * (kvw + 4 * feat),
            bytes_accessed=2 * (tokens * kvw + d * kvw + bands_dev * feat * d),
            transcendentals=0,
        ),
        compiler_params=pltpu.CompilerParams(vmem_limit_bytes=24 << 20),
        name="keys_values",
    )(*scalars, *args)


def time_kernel(parts, resident, tparts, q_ref, stream_ref, *refs):
    kv_refs, refs = refs[:parts], refs[parts:]
    wo_ref, w1_ref, w2_ref, out_ref, normed_ref, att_ref, hid_ref = refs
    frames = q_ref.shape[1]
    d = stream_ref.shape[-1]
    steps = tparts * BSTEP
    band0 = pl.program_id(0) * steps
    kv0 = band0 if resident else 0
    for c in range(CHUNKS):
        lo = QW + c * PER * VPAD

        def keyed(b, start, width):
            parts = [r[kv0 + b, ..., start : start + width].reshape(-1, width) for r in kv_refs]
            return jnp.concatenate(parts, axis=0)

        for b0 in range(0, steps, BATCH):
            ids = range(b0, b0 + BATCH)
            outs = attend(
                [q_ref[band0 + b, :, c * CW : (c + 1) * CW] for b in ids],
                [keyed(b, c * CW, CW) for b in ids],
                [keyed(b, lo, PER * VPAD) for b in ids],
            )
            for b, out in zip(ids, outs):
                att_ref[b * frames : (b + 1) * frames, c * PER * VPAD : (c + 1) * PER * VPAD] = out
    stream = stream_ref[pl.ds(band0, steps)].reshape(steps * frames, d).astype(F32)
    out = finish(stream, att_ref[...], wo_ref.at[0], w1_ref.at[0], w2_ref.at[0], hid_ref)
    rows = BSTEP * frames
    row = lax.broadcasted_iota(jnp.int32, (rows, rows), 0)
    col = lax.broadcasted_iota(jnp.int32, (rows, rows), 1)
    turn = jnp.where(col == (row % BSTEP) * frames + row // BSTEP, 1.0, 0.0).astype(BF)
    out = out.astype(BF)
    turned = [mm(turn, out[p * rows : (p + 1) * rows]) for p in range(tparts)]
    for p in range(tparts):
        out_ref[pl.program_id(0) * tparts + p] = turned[p].astype(BF)
        normed_ref[pl.program_id(0) * tparts + p] = rms(turned[p])


def time_layer(q, stream, kvs, resident, wo, ff_in, ff_out):
    bands_dev, frames, d = stream.shape
    ff = ff_in.shape[-1]
    tparts = TPARTS if resident else 1

    def kv_spec(a):
        if resident:
            return ONCHIP
        return pl.BlockSpec((tparts * BSTEP,) + a.shape[1:], lambda i: (i,) + (0,) * (len(a.shape) - 1))

    tokens = bands_dev * frames
    out_shape = jax.ShapeDtypeStruct((bands_dev // BSTEP, frames * BSTEP, d), BF)
    return pl.pallas_call(
        functools.partial(time_kernel, len(kvs), resident, tparts),
        grid=(bands_dev // (tparts * BSTEP),),
        in_specs=[ONCHIP] * 2 + [kv_spec(a) for a in kvs] + [ONCHIP] * 3,
        out_specs=[ONCHIP] * 2,
        out_shape=[out_shape] * 2,
        scratch_shapes=[
            pltpu.VMEM((tparts * BSTEP * frames, VW), BF),
            pltpu.VMEM((tparts * BSTEP * frames, ff), BF),
        ],
        cost_estimate=pl.CostEstimate(
            flops=4 * tokens * d * (ff + d), bytes_accessed=16 * tokens * d, transcendentals=0
        ),
        compiler_params=pltpu.CompilerParams(vmem_limit_bytes=(16 if resident else 56) << 20),
        name="time_layer",
    )(q, stream, *kvs, wo, ff_in, ff_out)


FSTEP = 16


def band_table(table_ref, which, parts):
    bands = parts * BSTEP
    t = table_ref[pl.ds(pl.multiple_of(which * bands, bands), bands), :]
    t = t.reshape(parts, 1, BSTEP, 2 * LANES)
    return jnp.broadcast_to(t, (parts, FSTEP, BSTEP, 2 * LANES)).reshape(-1, 2 * LANES)


def frame_rows(x, f, parts):
    step = x.shape[0] // parts
    pieces = [x[p * step + f * BSTEP : p * step + (f + 1) * BSTEP] for p in range(parts)]
    return jnp.concatenate(pieces, axis=0)


def own_kernel(table_ref, own_ref, wq_ref, wkv_ref, out_ref):
    parts, _, d = own_ref.shape
    rows = FSTEP * BSTEP
    here = pl.ds(pl.multiple_of(pl.program_id(0) * rows, rows), rows)
    n_own = own_ref[:, here, :].reshape(parts * rows, d)
    kv = mm(n_own, wkv_ref[1])
    q = mm(n_own, wq_ref[1])
    table = band_table(table_ref, lax.axis_index("head"), parts)
    scaled = table * (HEAD_DIM**-0.5 * math.log2(math.e))
    values = [rotated(q, scaled, c) for c in range(CHUNKS)]
    values += [rotated(kv, table, c) for c in range(CHUNKS)] + [kv[:, QW:]]
    at = 0
    for value in values:
        width = value.shape[1]
        for f in range(FSTEP):
            frame = pl.program_id(0) * FSTEP + f
            out_ref[frame, :, at : at + width] = frame_rows(value, f, parts).astype(BF)
        at += width


def own_projections(own, table, wq, wkv):
    parts, rows, d = own.shape
    frames, bands = rows // BSTEP, parts * BSTEP
    width = 2 * QW + VW
    return pl.pallas_call(
        own_kernel,
        grid=(frames // FSTEP,),
        in_specs=[ONCHIP] * 4,
        out_specs=ONCHIP,
        out_shape=jax.ShapeDtypeStruct((frames, bands, width), BF),
        cost_estimate=pl.CostEstimate(
            flops=2 * frames * bands * d * width,
            bytes_accessed=4 * frames * bands * width,
            transcendentals=0,
        ),
        compiler_params=pltpu.CompilerParams(vmem_limit_bytes=16 << 20),
        name="own_projections",
    )(table, own, wq, wkv)


def band_kernel(table_ref, stream_ref, own_ref, far_ref, *refs):
    wkv_ref, wo_ref, w1_ref, w2_ref, out_ref, att_ref, hid_ref = refs
    parts, _, d = stream_ref.shape
    bands = parts * BSTEP
    rows = FSTEP * BSTEP
    here = pl.ds(pl.multiple_of(pl.program_id(0) * rows, rows), rows)
    first = pl.program_id(0) * FSTEP
    kv = mm(far_ref[:, here, :].reshape(parts * rows, d), wkv_ref[1])
    table = band_table(table_ref, 1 - lax.axis_index("head"), parts)
    for c in range(CHUNKS):
        keys = rotated(kv, table, c)
        lo, wide = QW + c * PER * VPAD, PER * VPAD
        values = kv[:, lo : lo + wide]

        def joined(x, f, start):
            ours = own_ref[first + f, :, start : start + x.shape[1]]
            return jnp.concatenate([ours, frame_rows(x, f, parts).astype(BF)], axis=0)

        for f0 in range(0, FSTEP, BATCH):
            ids = range(f0, f0 + BATCH)
            outs = attend(
                [own_ref[first + f, :, c * CW : (c + 1) * CW] for f in ids],
                [joined(keys, f, QW + c * CW) for f in ids],
                [joined(values, f, QW + lo) for f in ids],
            )
            for f, out in zip(ids, outs):
                att_ref[f * bands : (f + 1) * bands, c * wide : (c + 1) * wide] = out
    stream = stream_ref[:, here, :].reshape(parts * rows, d).astype(F32)
    stream = jnp.concatenate([frame_rows(stream, f, parts) for f in range(FSTEP)], axis=0)
    out = finish(stream, att_ref[...], wo_ref.at[1], w1_ref.at[1], w2_ref.at[1], hid_ref)
    out_ref[...] = out.astype(BF).reshape(out_ref.shape)


def band_layer(stream, own, far, table, wkv, wo, ff_in, ff_out):
    parts, rows, d = stream.shape
    frames, bands = rows // BSTEP, parts * BSTEP
    ff = ff_in.shape[-1]
    tokens = bands * frames
    return pl.pallas_call(
        band_kernel,
        grid=(frames // FSTEP,),
        in_specs=[ONCHIP] * 8,
        out_specs=pl.BlockSpec((FSTEP, bands, d), lambda i: (i, 0, 0)),
        scratch_shapes=[
            pltpu.VMEM((bands * FSTEP, VW), BF),
            pltpu.VMEM((bands * FSTEP, ff), BF),
        ],
        out_shape=jax.ShapeDtypeStruct((frames, bands, d), BF),
        cost_estimate=pl.CostEstimate(
            flops=4 * tokens * d * (ff + 3 * d), bytes_accessed=16 * tokens * d, transcendentals=0
        ),
        compiler_params=pltpu.CompilerParams(vmem_limit_bytes=28 << 20),
        name="band_layer",
    )(table, stream, own, far, wkv, wo, ff_in, ff_out)


def per_device(n, spectrogram, band_lengths, band_weight, attn_weights, ff_in, ff_out):
    frames, _, bins = spectrogram.shape
    bands_dev = band_weight.shape[0]
    order = list(range(0, n, 2)) + [i for i in range(n - 1, -1, -1) if i % 2]
    spot = {t: i for i, t in enumerate(order)}
    after = {t: order[(spot[t] + 1) % n] for t in order}
    before = {t: order[(spot[t] - 1) % n] for t in order}
    steps = n // 2
    resident = 2 * bands_dev * n * frames * (QW + VW) <= KV_BYTES
    table = jnp.asarray(tables(n * frames))
    positions = jnp.asarray(tables(2 * bands_dev))
    ring = [(2 * t, 2 * after[t]) for t in range(n)] + [
        (2 * t + 1, 2 * before[t] + 1) for t in range(n)
    ]
    swap = [(0, 1), (1, 0)]

    block = spectrogram.transpose(1, 0, 2).reshape(CH * frames, bins)
    near = lax.ppermute(block, ("tm", "head"), ring)
    wq, wkv, wo = prep(attn_weights)
    project = functools.partial(keys_values, n)
    weights = (resident, band_lengths, table, band_weight, wkv)
    kv, q, stream, starts = project([block], ((0, 0),), *weights, wq=wq)
    near, kv = lax.optimization_barrier((near, kv))
    kvs, late = [kv], None
    for s in range(1, steps + 1):
        xs, slots = [near], [(s, 0)]
        if late is not None:
            xs.append(late)
            slots.append((s - 1, 1))
        if 2 * s != n:
            late = lax.ppermute(near, "head", swap)
        if s < steps:
            near = lax.ppermute(near, ("tm", "head"), ring)
        (kv,) = project(xs, tuple(slots), *weights, starts)
        near, late, kv = lax.optimization_barrier((near, late, kv))
        kvs.append(kv)
    if 2 * steps != n:
        kvs += project([late], ((steps, 1),), *weights, starts)
    stream, own = time_layer(q, stream, kvs, resident, wo, ff_in, ff_out)
    far = lax.ppermute(own, "head", swap)
    own = own_projections(own, positions, wq, wkv)
    return band_layer(stream, own, far, positions, wkv, wo, ff_in, ff_out)


def solution(mesh):
    return jax.shard_map(
        functools.partial(per_device, mesh.shape["tm"]),
        mesh=mesh,
        in_specs=(P(("groups", "tm"), None, None), P(), P("head", None, None), P(), P(), P()),
        out_specs=P(("groups", "tm"), "head", None),
        check_vma=False,
    )
```

```python
import functools
import math

import jax
import jax.numpy as jnp
import numpy as np
from jax import lax
from jax.experimental import pallas as pl
from jax.experimental.pallas import tpu as pltpu
from jax.sharding import PartitionSpec as P

HEADS = 8
HEAD_DIM = 48
MAXW = 32
CH = 4
HALF = HEAD_DIM // 2
HPAD = 32
VPAD = 64
LANES = 128
PER = LANES // HPAD
CHUNKS = HEADS // PER
QW = 2 * HEADS * HPAD
VW = HEADS * VPAD
GROUP = LANES // MAXW
CW = 2 * LANES
BSTEP = 8
KSTEP = 16
TPARTS = 2
BATCH = 16
BF = jnp.bfloat16
F32 = jnp.float32


ONCHIP = pl.BlockSpec(memory_space=pltpu.VMEM)
KV_BYTES = 20 << 20


def mm(a, b):
    return jnp.dot(a, b, preferred_element_type=F32)


def mm_nt(a, b):
    return lax.dot_general(a, b, (((1,), (1,)), ((), ())), preferred_element_type=F32)


def rms(x):
    return (x * lax.rsqrt(jnp.mean(x * x, axis=-1, keepdims=True) + 1e-06)).astype(BF)


def tables(count):
    freq = 10000.0 ** (-np.arange(HALF, dtype=np.float64) / HALF)
    angle = np.arange(count, dtype=np.float64)[:, None] * freq
    pad = ((0, 0), (0, HPAD - HALF))
    cosine = np.tile(np.pad(np.cos(angle), pad), (1, PER))
    sine = np.tile(np.pad(np.sin(angle), pad), (1, PER))
    return np.concatenate([cosine, sine], axis=1).astype(np.float32)


def rotated(x, table, c):
    period = table.shape[0]
    u = x[:, c * CW : c * CW + LANES].reshape(-1, period, LANES)
    w = x[:, c * CW + LANES : (c + 1) * CW].reshape(-1, period, LANES)
    cosine, sine = table[None, :, :LANES], table[None, :, LANES:]
    first = (u * cosine - w * sine).reshape(-1, LANES)
    second = (w * cosine + u * sine).reshape(-1, LANES)
    return jnp.concatenate([first, second], axis=1)


def gelu(x):
    return 0.5 * x * (1.0 + lax.erf(x * math.sqrt(0.5)))


def finish(stream, att, wo, w1, w2, hid_ref):
    mid = stream + mm(att, wo[...])
    normed = rms(mid)
    width = w1.shape[-1]
    step = 256
    for j in range(0, width, step):
        hid_ref[:, j : j + step] = gelu(mm(normed, w1[:, j : j + step])).astype(BF)
    return mid + mm(hid_ref[...], w2[...])


def attend(queries, keys, values):
    m = queries[0].shape[0]
    own = (lax.broadcasted_iota(jnp.int32, (1, CW), 1) % LANES) // HPAD
    vlane = lax.broadcasted_iota(jnp.int32, (1, PER * VPAD), 1) // VPAD
    stacked = [
        jnp.concatenate([jnp.where(own == h, q, jnp.zeros_like(q)) for h in range(PER)], axis=0)
        for q in queries
    ]
    scores = [mm_nt(q, k) for q, k in zip(stacked, keys)]
    highest = [jnp.max(s, axis=-1, keepdims=True) for s in scores]
    powers = [jnp.exp2(s - h) for s, h in zip(scores, highest)]
    sums = [jnp.sum(p, axis=-1, keepdims=True) for p in powers]
    mixed = [mm(p.astype(BF), v) for p, v in zip(powers, values)]
    outs = []
    for r, total in zip(mixed, sums):
        r = r * (1.0 / total)
        out = r[:m]
        for h in range(1, PER):
            out = jnp.where(vlane == h, r[h * m : (h + 1) * m], out)
        outs.append(out.astype(BF))
    return outs


def prep_kernel(w_ref, wq_ref, wkv_ref, wo_ref):
    layers, _, d, _ = w_ref.shape
    share = d // CHUNKS
    span = -(-share // LANES) * LANES
    for c in range(CHUNKS):
        low = min(c * share // LANES * LANES, d - span)
        shift = c * share - low
        row = lax.broadcasted_iota(jnp.int32, (span, CW), 0)
        col = lax.broadcasted_iota(jnp.int32, (span, CW), 1)
        inner = col % HPAD
        source = (col % LANES) // HPAD * HEAD_DIM + col // LANES * HALF + inner + shift
        pick = jnp.where((row == source) & (inner < HALF), 1.0, 0.0).astype(BF)
        inner = col % VPAD
        source = col // VPAD * HEAD_DIM + inner + shift
        vpick = jnp.where((row == source) & (inner < HEAD_DIM), 1.0, 0.0).astype(BF)
        row = lax.broadcasted_iota(jnp.int32, (CW, span), 0)
        col = lax.broadcasted_iota(jnp.int32, (CW, span), 1)
        inner = row % VPAD
        source = row // VPAD * HEAD_DIM + inner + shift
        opick = jnp.where((col == source) & (inner < HEAD_DIM), 1.0, 0.0).astype(BF)
        to = slice(c * CW, (c + 1) * CW)
        for i in range(layers):
            part = slice(low, low + span)
            wq_ref[i, :, to] = mm(w_ref[i, 0, :, part], pick).astype(BF)
            wkv_ref[i, :, to] = mm(w_ref[i, 1, :, part], pick).astype(BF)
            at = slice(QW + c * CW, QW + (c + 1) * CW)
            wkv_ref[i, :, at] = mm(w_ref[i, 2, :, part], vpick).astype(BF)
            wo_ref[i, to, :] = mm(opick, w_ref[i, 3, part, :]).astype(BF)


def prep(attn_weights):
    layers, _, d, _ = attn_weights.shape
    return pl.pallas_call(
        prep_kernel,
        in_specs=[ONCHIP],
        out_specs=[ONCHIP] * 3,
        out_shape=[
            jax.ShapeDtypeStruct((layers, d, QW), BF),
            jax.ShapeDtypeStruct((layers, d, QW + VW), BF),
            jax.ShapeDtypeStruct((layers, VW, d), BF),
        ],
        cost_estimate=pl.CostEstimate(
            flops=layers * 8 * d * d * QW, bytes_accessed=layers * 16 * d * d, transcendentals=0
        ),
        compiler_params=pltpu.CompilerParams(vmem_limit_bytes=16 << 20),
        name="prep",
    )(attn_weights)


def embed(x_refs, weight_ref, band0, lens, starts):
    rows, bins = x_refs[0].shape
    frames = rows // CH
    lane = lax.broadcasted_iota(jnp.int32, (1, LANES), 1)
    inner = lane % MAXW
    bin_row = lax.broadcasted_iota(jnp.int32, (2 * LANES, LANES), 0)
    groups = [range(b, b + GROUP) for b in range(0, KSTEP, GROUP)]
    picked = []
    for ids in groups:
        base = jnp.minimum(starts[ids[0]] // LANES, (bins - 2 * LANES) // LANES) * LANES
        base = pl.multiple_of(base, LANES)
        target = jnp.full((1, LANES), -1, jnp.int32)
        for k, b in enumerate(ids):
            mine = (lane // MAXW == k) & (inner < lens[b])
            target = jnp.where(mine, starts[b] - base + inner, target)
        select = jnp.where(bin_row == target, 1.0, 0.0).astype(BF)
        window = jnp.concatenate([x[:, pl.ds(base, 2 * LANES)] for x in x_refs], axis=0)
        picked.append(mm(window, select))
    scales, lefts = [], []
    for ids, features in zip(groups, picked):
        narrow = features.astype(BF)
        square = features * features
        scale, left = [], []
        for i in range(len(x_refs)):
            spots = [slice(i * rows + c * frames, i * rows + (c + 1) * frames) for c in range(CH)]
            total = square[spots[0]]
            for spot in spots[1:]:
                total = total + square[spot]
            for k, b in enumerate(ids):
                mine = lane // MAXW == k
                mean = jnp.sum(jnp.where(mine, total, 0.0), axis=-1, keepdims=True) / (
                    (CH * lens[b]).astype(F32)
                )
                scale.append(lax.rsqrt(jnp.maximum(mean, 0.25)))
                kept = [jnp.where(mine, narrow[spot], jnp.zeros((), BF)) for spot in spots]
                left.append(jnp.concatenate(kept, axis=1))
        scales.append(jnp.concatenate(scale, axis=0))
        lefts.append(jnp.concatenate(left, axis=0))
    streams = []
    for ids, left, scale in zip(groups, lefts, scales):
        weight = jnp.concatenate(
            [weight_ref[band0 + b, c * MAXW : (c + 1) * MAXW, :] for c in range(CH) for b in ids],
            axis=0,
        )
        streams.append(mm(left, weight) * scale)
    return jnp.concatenate(streams, axis=0)


def source_block(n, step, side):
    t, h = lax.axis_index("tm"), lax.axis_index("head")
    spot = jnp.where(t % 2 == 0, t // 2, n - 1 - t // 2)
    back = (h == 0) == (side == 0)
    spot = lax.rem(jnp.where(back, spot - step, spot + step) + n, n)
    return jnp.where(spot < (n + 1) // 2, 2 * spot, 2 * (n - 1 - spot) + 1)


def kv_kernel(n, blocks, slots, with_q, resident, lens_ref, *refs):
    if with_q:
        *refs, starts_ref = refs

        @pl.when(pl.program_id(0) == 0)
        def _():
            start = jnp.int32(0)
            for b in range(lens_ref.shape[0]):
                starts_ref[b] = start
                start = start + lens_ref[b]

    else:
        starts_ref, *refs = refs
    table_ref, *refs = refs
    x_refs, refs = refs[:blocks], refs[blocks:]
    weight_ref, wkv_ref, *refs = refs
    if with_q:
        wq_ref, *refs = refs
    kv_ref = refs[0]
    bands_dev = weight_ref.shape[0]
    frames = x_refs[0].shape[0] // CH
    band0 = pl.program_id(0) * KSTEP
    first = lax.axis_index("head") * bands_dev + band0
    lens = [lens_ref[first + b] for b in range(KSTEP)]
    starts = [starts_ref[first + b] for b in range(KSTEP)]
    stream = embed(x_refs, weight_ref, band0, lens, starts)
    normed = rms(stream)
    kv = mm(normed, wkv_ref[0])
    places = [pl.multiple_of(source_block(n, *slot) * frames, frames) for slot in slots]
    table = jnp.concatenate(
        [table_ref[pl.ds(p, frames), :] for p in places for _ in range(GROUP)], axis=0
    )

    def put(ref, base, cols, value):
        width = value.shape[1]
        value = value.reshape(KSTEP // GROUP, blocks, GROUP, frames, width)
        for g in range(KSTEP // GROUP):
            bands = pl.ds(base + g * GROUP, GROUP)
            if len(ref.shape) == 3:
                ref[bands, :, cols : cols + width] = value[g, 0]
                continue
            for i in range(blocks):
                ref[bands, i, :, cols : cols + width] = value[g, i]

    base = band0 if resident else 0
    for c in range(CHUNKS):
        put(kv_ref, base, c * CW, rotated(kv, table, c).astype(BF))
    put(kv_ref, base, QW, kv[:, QW:].astype(BF))
    if with_q:
        q_ref, stream_ref = refs[1:3]

        def first_block(x):
            x = x.reshape(KSTEP // GROUP, blocks, GROUP * frames, x.shape[1])[:, 0]
            return x.reshape(KSTEP * frames, x.shape[2])

        q = mm(first_block(normed), wq_ref[0])
        scaled = table[: GROUP * frames] * (HEAD_DIM**-0.5 * math.log2(math.e))
        here = pl.ds(band0, KSTEP)
        for c in range(CHUNKS):
            turned = rotated(q, scaled, c).astype(BF).reshape(KSTEP, frames, CW)
            q_ref[here, :, c * CW : (c + 1) * CW] = turned
        stream_ref[here] = first_block(stream).astype(BF).reshape(KSTEP, frames, stream.shape[1])


def keys_values(n, xs, slots, resident, lens, table, band_weight, wkv, starts=None, wq=None):
    blocks = len(xs)
    with_q = wq is not None
    rows, bins = xs[0].shape
    frames = rows // CH
    bands_dev, feat, d = band_weight.shape
    kvw = QW + VW
    lead = () if blocks == 1 else (blocks,)
    zeros = (0,) * (len(lead) + 2)
    out_shape = [jax.ShapeDtypeStruct((bands_dev,) + lead + (frames, kvw), BF)]
    out_specs = [
        ONCHIP
        if resident
        else pl.BlockSpec((KSTEP,) + lead + (frames, kvw), lambda i, *_: (i,) + zeros)
    ]
    args = [table, *xs, band_weight, wkv]
    if with_q:
        args.append(wq)
        for width in (QW, d):
            out_shape.append(jax.ShapeDtypeStruct((bands_dev, frames, width), BF))
            out_specs.append(ONCHIP)
        out_shape.append(jax.ShapeDtypeStruct(lens.shape, jnp.int32))
        out_specs.append(pl.BlockSpec(memory_space=pltpu.SMEM))
    scalars = [lens] if with_q else [lens, starts]
    tokens = blocks * frames * bands_dev
    return pl.pallas_call(
        functools.partial(kv_kernel, n, blocks, slots, with_q, resident),
        grid_spec=pltpu.PrefetchScalarGridSpec(
            num_scalar_prefetch=len(scalars),
            grid=(bands_dev // KSTEP,),
            in_specs=[ONCHIP] * len(args),
            out_specs=out_specs,
        ),
        out_shape=out_shape,
        cost_estimate=pl.CostEstimate(
            flops=2 * tokens * d * (kvw + 4 * feat),
            bytes_accessed=2 * (tokens * kvw + d * kvw + bands_dev * feat * d),
            transcendentals=0,
        ),
        compiler_params=pltpu.CompilerParams(vmem_limit_bytes=24 << 20),
        name="keys_values",
    )(*scalars, *args)


def time_kernel(parts, resident, tparts, q_ref, stream_ref, *refs):
    kv_refs, refs = refs[:parts], refs[parts:]
    wo_ref, w1_ref, w2_ref, out_ref, normed_ref, att_ref, hid_ref = refs
    frames = q_ref.shape[1]
    d = stream_ref.shape[-1]
    steps = tparts * BSTEP
    band0 = pl.program_id(0) * steps
    kv0 = band0 if resident else 0
    for c in range(CHUNKS):
        lo = QW + c * PER * VPAD

        def keyed(b, start, width):
            parts = [r[kv0 + b, ..., start : start + width].reshape(-1, width) for r in kv_refs]
            return jnp.concatenate(parts, axis=0)

        for b0 in range(0, steps, BATCH):
            ids = range(b0, min(b0 + BATCH, steps))
            outs = attend(
                [q_ref[band0 + b, :, c * CW : (c + 1) * CW] for b in ids],
                [keyed(b, c * CW, CW) for b in ids],
                [keyed(b, lo, PER * VPAD) for b in ids],
            )
            for b, out in zip(ids, outs):
                att_ref[b * frames : (b + 1) * frames, c * PER * VPAD : (c + 1) * PER * VPAD] = out
    stream = stream_ref[pl.ds(band0, steps)].reshape(steps * frames, d).astype(F32)
    out = finish(stream, att_ref[...], wo_ref.at[0], w1_ref.at[0], w2_ref.at[0], hid_ref)
    rows = BSTEP * frames
    row = lax.broadcasted_iota(jnp.int32, (rows, rows), 0)
    col = lax.broadcasted_iota(jnp.int32, (rows, rows), 1)
    turn = jnp.where(col == (row % BSTEP) * frames + row // BSTEP, 1.0, 0.0).astype(BF)
    out = out.astype(BF)
    turned = [mm(turn, out[p * rows : (p + 1) * rows]) for p in range(tparts)]
    for p in range(tparts):
        out_ref[pl.program_id(0) * tparts + p] = turned[p].astype(BF)
        normed_ref[pl.program_id(0) * tparts + p] = rms(turned[p])


def time_layer(q, stream, kvs, resident, wo, ff_in, ff_out):
    bands_dev, frames, d = stream.shape
    ff = ff_in.shape[-1]
    tparts = TPARTS if resident else 1

    def kv_spec(a):
        if resident:
            return ONCHIP
        return pl.BlockSpec((tparts * BSTEP,) + a.shape[1:], lambda i: (i,) + (0,) * (len(a.shape) - 1))

    tokens = bands_dev * frames
    out_shape = jax.ShapeDtypeStruct((bands_dev // BSTEP, frames * BSTEP, d), BF)
    return pl.pallas_call(
        functools.partial(time_kernel, len(kvs), resident, tparts),
        grid=(bands_dev // (tparts * BSTEP),),
        in_specs=[ONCHIP] * 2 + [kv_spec(a) for a in kvs] + [ONCHIP] * 3,
        out_specs=[ONCHIP] * 2,
        out_shape=[out_shape] * 2,
        scratch_shapes=[
            pltpu.VMEM((tparts * BSTEP * frames, VW), BF),
            pltpu.VMEM((tparts * BSTEP * frames, ff), BF),
        ],
        cost_estimate=pl.CostEstimate(
            flops=4 * tokens * d * (ff + d), bytes_accessed=16 * tokens * d, transcendentals=0
        ),
        compiler_params=pltpu.CompilerParams(vmem_limit_bytes=(16 if resident else 56) << 20),
        name="time_layer",
    )(q, stream, *kvs, wo, ff_in, ff_out)


FSTEP = 16


def band_table(table_ref, which, parts):
    bands = parts * BSTEP
    t = table_ref[pl.ds(pl.multiple_of(which * bands, bands), bands), :]
    t = t.reshape(parts, 1, BSTEP, 2 * LANES)
    return jnp.broadcast_to(t, (parts, FSTEP, BSTEP, 2 * LANES)).reshape(-1, 2 * LANES)


def frame_rows(x, f, parts):
    step = x.shape[0] // parts
    pieces = [x[p * step + f * BSTEP : p * step + (f + 1) * BSTEP] for p in range(parts)]
    return jnp.concatenate(pieces, axis=0)


def own_kernel(table_ref, own_ref, wq_ref, wkv_ref, out_ref):
    parts, _, d = own_ref.shape
    rows = FSTEP * BSTEP
    here = pl.ds(pl.multiple_of(pl.program_id(0) * rows, rows), rows)
    n_own = own_ref[:, here, :].reshape(parts * rows, d)
    kv = mm(n_own, wkv_ref[1])
    q = mm(n_own, wq_ref[1])
    table = band_table(table_ref, lax.axis_index("head"), parts)
    scaled = table * (HEAD_DIM**-0.5 * math.log2(math.e))
    values = [rotated(q, scaled, c) for c in range(CHUNKS)]
    values += [rotated(kv, table, c) for c in range(CHUNKS)] + [kv[:, QW:]]
    at = 0
    for value in values:
        width = value.shape[1]
        for f in range(FSTEP):
            frame = pl.program_id(0) * FSTEP + f
            out_ref[frame, :, at : at + width] = frame_rows(value, f, parts).astype(BF)
        at += width


def own_projections(own, table, wq, wkv):
    parts, rows, d = own.shape
    frames, bands = rows // BSTEP, parts * BSTEP
    width = 2 * QW + VW
    return pl.pallas_call(
        own_kernel,
        grid=(frames // FSTEP,),
        in_specs=[ONCHIP] * 4,
        out_specs=ONCHIP,
        out_shape=jax.ShapeDtypeStruct((frames, bands, width), BF),
        cost_estimate=pl.CostEstimate(
            flops=2 * frames * bands * d * width,
            bytes_accessed=4 * frames * bands * width,
            transcendentals=0,
        ),
        compiler_params=pltpu.CompilerParams(vmem_limit_bytes=16 << 20),
        name="own_projections",
    )(table, own, wq, wkv)


def band_kernel(table_ref, stream_ref, own_ref, far_ref, *refs):
    wkv_ref, wo_ref, w1_ref, w2_ref, out_ref, att_ref, hid_ref = refs
    parts, _, d = stream_ref.shape
    bands = parts * BSTEP
    rows = FSTEP * BSTEP
    here = pl.ds(pl.multiple_of(pl.program_id(0) * rows, rows), rows)
    first = pl.program_id(0) * FSTEP
    kv = mm(far_ref[:, here, :].reshape(parts * rows, d), wkv_ref[1])
    table = band_table(table_ref, 1 - lax.axis_index("head"), parts)
    for c in range(CHUNKS):
        keys = rotated(kv, table, c)
        lo, wide = QW + c * PER * VPAD, PER * VPAD
        values = kv[:, lo : lo + wide]

        def joined(x, f, start):
            ours = own_ref[first + f, :, start : start + x.shape[1]]
            return jnp.concatenate([ours, frame_rows(x, f, parts).astype(BF)], axis=0)

        for f0 in range(0, FSTEP, BATCH):
            ids = range(f0, f0 + BATCH)
            outs = attend(
                [own_ref[first + f, :, c * CW : (c + 1) * CW] for f in ids],
                [joined(keys, f, QW + c * CW) for f in ids],
                [joined(values, f, QW + lo) for f in ids],
            )
            for f, out in zip(ids, outs):
                att_ref[f * bands : (f + 1) * bands, c * wide : (c + 1) * wide] = out
    stream = stream_ref[:, here, :].reshape(parts * rows, d).astype(F32)
    stream = jnp.concatenate([frame_rows(stream, f, parts) for f in range(FSTEP)], axis=0)
    out = finish(stream, att_ref[...], wo_ref.at[1], w1_ref.at[1], w2_ref.at[1], hid_ref)
    out_ref[...] = out.astype(BF).reshape(out_ref.shape)


def band_layer(stream, own, far, table, wkv, wo, ff_in, ff_out):
    parts, rows, d = stream.shape
    frames, bands = rows // BSTEP, parts * BSTEP
    ff = ff_in.shape[-1]
    tokens = bands * frames
    return pl.pallas_call(
        band_kernel,
        grid=(frames // FSTEP,),
        in_specs=[ONCHIP] * 8,
        out_specs=pl.BlockSpec((FSTEP, bands, d), lambda i: (i, 0, 0)),
        scratch_shapes=[
            pltpu.VMEM((bands * FSTEP, VW), BF),
            pltpu.VMEM((bands * FSTEP, ff), BF),
        ],
        out_shape=jax.ShapeDtypeStruct((frames, bands, d), BF),
        cost_estimate=pl.CostEstimate(
            flops=4 * tokens * d * (ff + 3 * d), bytes_accessed=16 * tokens * d, transcendentals=0
        ),
        compiler_params=pltpu.CompilerParams(vmem_limit_bytes=28 << 20),
        name="band_layer",
    )(table, stream, own, far, wkv, wo, ff_in, ff_out)


def per_device(n, spectrogram, band_lengths, band_weight, attn_weights, ff_in, ff_out):
    frames, _, bins = spectrogram.shape
    bands_dev = band_weight.shape[0]
    order = list(range(0, n, 2)) + [i for i in range(n - 1, -1, -1) if i % 2]
    spot = {t: i for i, t in enumerate(order)}
    after = {t: order[(spot[t] + 1) % n] for t in order}
    before = {t: order[(spot[t] - 1) % n] for t in order}
    steps = n // 2
    resident = 2 * bands_dev * n * frames * (QW + VW) <= KV_BYTES
    table = jnp.asarray(tables(n * frames))
    positions = jnp.asarray(tables(2 * bands_dev))
    ring = [(2 * t, 2 * after[t]) for t in range(n)] + [
        (2 * t + 1, 2 * before[t] + 1) for t in range(n)
    ]
    swap = [(0, 1), (1, 0)]

    block = spectrogram.transpose(1, 0, 2).reshape(CH * frames, bins)
    near = lax.ppermute(block, ("tm", "head"), ring)
    wq, wkv, wo = prep(attn_weights)
    near, wkv = lax.optimization_barrier((near, wkv))
    project = functools.partial(keys_values, n)
    weights = (resident, band_lengths, table, band_weight, wkv)
    kvs, late = [], block
    for s in range(1, steps + 1):
        xs, slots = [late, near], [(s - 1, 1), (s, 0)]
        if 2 * s != n:
            late = lax.ppermute(near, "head", swap)
        if s < steps:
            near = lax.ppermute(near, ("tm", "head"), ring)
        if s == 1:
            kv, q, stream, starts = project(xs, tuple(slots), *weights, wq=wq)
        else:
            (kv,) = project(xs, tuple(slots), *weights, starts)
        near, late, kv = lax.optimization_barrier((near, late, kv))
        kvs.append(kv)
    if 2 * steps != n:
        kvs += project([late], ((steps, 1),), *weights, starts)
    stream, own = time_layer(q, stream, kvs, resident, wo, ff_in, ff_out)
    far = lax.ppermute(own, "head", swap)
    own = own_projections(own, positions, wq, wkv)
    return band_layer(stream, own, far, positions, wkv, wo, ff_in, ff_out)


def solution(mesh):
    return jax.shard_map(
        functools.partial(per_device, mesh.shape["tm"]),
        mesh=mesh,
        in_specs=(P(("groups", "tm"), None, None), P(), P("head", None, None), P(), P(), P()),
        out_specs=P(("groups", "tm"), "head", None),
        check_vma=False,
    )
```
